128 devices in a mesh: section: 2 (over x_hi), seq: 16 (over z, y), mp: 4 (over x_lo, core).
Axes of the slice: x: 4 (x_hi: 2, x_lo: 2; x = x_hi * 2 + x_lo), y: 4, z: 4, core: 2. Of those that a mesh axis runs over, the one named last changes fastest.
Arguments:
- video: bfloat16 [2, 4, 128, 3072], P(None, None, 'seq'), may hold values from -6 to 6
- text: bfloat16 [2, 128, 3072], P(None, 'seq'), may hold values from -6 to 6
- patch_lengths: int32 [2, 4], replicated, may hold values from 1 to 128, 384 in all within a row
- text_len: int32 [2], replicated, may hold values from 64 to 128, as said below
- timestep: int32 [1], replicated, may hold values from 0 to 999
- w_mod: bfloat16 [2, 512, 9216], P('section', None, 'mp'), may hold values from -0.25 to 0.25
- w_qkv: bfloat16 [2, 3072, 3, 3072], P('section', None, None, 'mp')
- w_out: bfloat16 [2, 3072, 3072], P('section', 'mp'), may hold values from -0.109375 to 0.109375
- stale_cache: bfloat16 [2, 2, 4, 128, 2, 3072], P('section', None, None, 'seq', None, 'mp'), may hold values from -6 to 6
Outputs:
- hidden_video: bfloat16 [2, 2, 4, 128, 3072], P('section', None, None, 'seq')
- hidden_text: bfloat16 [2, 2, 128, 3072], P('section', None, 'seq')
- cache_video: bfloat16 [2, 2, 4, 128, 2, 3072], P('section', None, None, 'seq', None, 'mp')
- cache_text: bfloat16 [2, 2, 128, 2, 3072], P('section', None, 'seq', None, 'mp')
The draws below stay inside these ranges and needn't reach their ends.
Inputs may be any that keep to these rules, and one draw needn't show every extreme that they name: `patch_lengths`: 4 patch lengths per request summing to 384; in every request the largest is 128. `text_len`: exactly one request has 128, every other fewer.
All inputs are finite; a program needn't handle non-finite values.
Results may differ from the reference program's by a relative error of at most 0.01.
Values may be sent and summed in bfloat16 or wider, within the bound.
No kernel may reach another device: no remote copies, remote signals or barrier semaphores. Data moves between devices by JAX's collectives and lax.ppermute only.
A program may use at most 192 MiB of HBM per device.

```python
import math
import jax
import jax.numpy as jnp
import numpy as np
from jax import lax

D = 3072
HEAD = 64
TE = 512
REQS = 2
NPATCH = 4
HD = 3072
PCAP = 128
VIDEO = 384
TEXT = 128


def draw_text_len(key, part):
    lengths = jax.random.randint(key, (REQS,), TEXT // 2, TEXT)
    chosen = jax.random.randint(jax.random.fold_in(key, 3), (), 0, REQS)
    return jnp.where(jnp.arange(REQS) == chosen, TEXT, lengths).astype(jnp.int32)


def draw_w_qkv(key, part):
    drawn = jax.random.normal(key, (2, D, 3, HD), jnp.float32) * D ** (-0.5)
    return drawn.astype(jnp.bfloat16)


def block_scale(rng, shape, shards, smallest, high):
    factor_of = 1.0
    for axis_at, blocks in shards:
        steps = jax.random.uniform(jax.random.fold_in(jax.random.fold_in(rng, 6), axis_at), (blocks,), jnp.float32, smallest / len(shards), high / len(shards))
        factor_of = factor_of * jnp.repeat(jnp.exp(steps), shape[axis_at] // blocks).reshape((-1,) + (1,) * (len(shape) - 1 - axis_at))
    return factor_of


def split_up(amount, total, reach, lean):
    portions = [(1 << 20) // math.isqrt(standing ** lean) + 1 for standing in range(2, amount + 1)]
    rest, holding = total - reach - (amount - 1), [1] * (amount - 1)
    while rest > 0:
        movable = [i for i in range(amount - 1) if holding[i] < reach]
        whole, remaining = sum([portions[i] for i in movable]), rest
        for i in movable:
            extra = min(reach - holding[i], max(1, remaining * portions[i] // whole), rest)
            holding[i] = holding[i] + extra
            rest = rest - extra
    return np.array([reach] + holding)


def uneven_parts(key, amount, total, limit, skew):
    if amount == 2:
        one = jax.random.randint(key, (), max(1, total - limit), min(limit, total - 1) + 1)
        return jnp.stack([one, total - one])
    sizes = jnp.asarray(split_up(amount, total, limit, skew), jnp.int32)
    twos = (amount - 1) // 2
    donor, taker = sizes[1:1 + 2 * twos:2], sizes[2:2 + 2 * twos:2]
    margin = jnp.minimum(donor - 1, limit - taker)
    shifted = jax.random.randint(jax.random.fold_in(key, 1), (twos,), 0, 1 << 20) % (margin + 1)
    sizes = sizes.at[1:1 + 2 * twos:2].set(donor - shifted).at[2:2 + 2 * twos:2].set(taker + shifted)
    return sizes[jax.random.permutation(jax.random.fold_in(key, 2), amount)]


def scatter_about(stream_key, extent, deviation, most, split=(), held_as=jnp.bfloat16):
    values = deviation * jax.random.normal(stream_key, extent, jnp.float32)
    if split:
        values = values * block_scale(stream_key, extent, split, -0.22, 0.18)
    return jnp.clip(values, -most, most).astype(held_as)


def setup_inputs(seed: int = 0) -> dict:
    arg_keys = jax.random.split(jax.random.key(seed), 10)
    video = scatter_about(arg_keys[0], (REQS, NPATCH, PCAP, D), 1.0, 6.0, ((2, 16),))
    text = scatter_about(arg_keys[1], (REQS, TEXT, D), 1.0, 6.0, ((1, 16),))
    patch_lengths = jax.vmap(lambda own: uneven_parts(own, NPATCH, VIDEO, PCAP, 2))(jax.random.split(arg_keys[2], REQS)).reshape((REQS, NPATCH)).astype(jnp.int32)
    text_len = draw_text_len(jax.random.fold_in(arg_keys[9], 71), 0)
    timestep = jax.random.randint(arg_keys[4], (1,), 0, 1000).astype(jnp.int32)
    w_mod = scatter_about(arg_keys[5], (2, TE, 3 * D), TE ** -0.5, 0.25, ((0, 2), (2, 4)))
    w_qkv = draw_w_qkv(jax.random.fold_in(arg_keys[9], 71), 0)
    w_out = scatter_about(arg_keys[7], (2, HD, D), HD ** -0.5, 0.109375, ((0, 2), (1, 4)))
    stale_cache = scatter_about(arg_keys[8], (2, REQS, NPATCH, PCAP, 2, HD), 1.0, 6.0, ((0, 2), (3, 16), (5, 4)))
    return {"video": video, "text": text, "patch_lengths": patch_lengths, "text_len": text_len, "timestep": timestep, "w_mod": w_mod, "w_qkv": w_qkv, "w_out": w_out, "stale_cache": stale_cache}


EPS = 1e-05
NEG = -1e+30

def modulation(timestep, weight):
    half_width = weight.shape[0] // 2
    frequency = jnp.exp(-math.log(10000.0) * jnp.arange(half_width, dtype=jnp.float32) / half_width)
    phases = timestep.astype(jnp.float32)[0] * frequency
    embedding = jnp.concatenate([jnp.cos(phases), jnp.sin(phases)])
    active = jax.nn.silu(embedding).astype(jnp.bfloat16)
    return jnp.dot(active[None, :], weight, preferred_element_type=jnp.float32)[0]

def normalize(token_rows, shift_vec, scale_vec):
    values = token_rows.astype(jnp.float32)
    center = values - lax.optimization_barrier(jnp.mean(values, axis=-1, keepdims=True))
    spread = lax.optimization_barrier(jnp.mean(center * center, axis=-1, keepdims=True))
    return (center * lax.rsqrt(spread + EPS) * (1.0 + scale_vec) + shift_vec).astype(jnp.bfloat16)

def masked_terms(queries, key_heads, value_heads, key_mask):
    scores = jnp.einsum('rqe,rke->rqk', queries.astype(jnp.float32), key_heads.astype(jnp.float32)) * HEAD ** (-0.5)
    top_score = lax.optimization_barrier(jnp.max(jnp.where(key_mask, scores, NEG), axis=-1))
    weights = jnp.where(key_mask, jnp.exp(scores - top_score[..., None]), 0.0)
    weight_sum = lax.optimization_barrier(jnp.sum(weights, axis=-1))
    accumulated = jnp.einsum('rqk,rke->rqe', weights.astype(jnp.bfloat16).astype(jnp.float32), value_heads.astype(jnp.float32))
    return (top_score, weight_sum, accumulated)

def apply_layer(video, text, weight_mod, weight_qkv, weight_out, stale, patch_lengths, text_len, timestep):
    requests, patches, capacity, model_width = video.shape
    text_slots = text.shape[1]
    modulated = modulation(timestep, weight_mod)
    shift_vec = modulated[:model_width]
    scale_vec = modulated[model_width:2 * model_width]
    gate_vec = modulated[2 * model_width:]
    token_rows = jnp.concatenate([video.reshape(requests, patches * capacity, model_width), text], axis=1)
    row_count = token_rows.shape[1]
    normed = normalize(token_rows, shift_vec, scale_vec)
    column_count = weight_out.shape[0]
    head_count = column_count // HEAD
    projected = jnp.dot(normed.reshape(-1, model_width), weight_qkv.reshape(model_width, 3 * column_count), preferred_element_type=jnp.float32)
    projected = projected.reshape(requests, row_count, 3, column_count).astype(jnp.bfloat16)

    def split_heads(array):
        return array.reshape(requests, array.shape[1], head_count, HEAD).transpose(2, 0, 1, 3)
    video_patch = jnp.repeat(jnp.arange(patches, dtype=jnp.int32), capacity)
    all_patch = jnp.concatenate([video_patch, jnp.zeros((text_slots,), jnp.int32)])
    slot_index = jnp.arange(capacity, dtype=jnp.int32)
    video_valid = (slot_index[None, None, :] < patch_lengths[:, :, None]).reshape(requests, -1)
    text_valid = jnp.arange(text_slots, dtype=jnp.int32)[None, :] < text_len[:, None]
    all_valid = jnp.concatenate([video_valid, text_valid], axis=1)
    fresh_mask = all_valid[:, None, :] & (all_patch[None, None, :] <= all_patch[None, :, None])
    stale_mask = video_valid[:, None, :] & (video_patch[None, None, :] > all_patch[None, :, None])
    stale_flat = stale.reshape(requests, patches * capacity, 2, column_count)

    def per_head(pieces):
        query_h, key_h, value_h, stale_key_h, stale_value_h = pieces
        fresh_top, fresh_sum, fresh_acc = masked_terms(query_h, key_h, value_h, fresh_mask)
        stale_top, stale_sum, stale_acc = masked_terms(query_h, stale_key_h, stale_value_h, stale_mask)
        top_score = jnp.maximum(fresh_top, stale_top)
        fresh_weight = jnp.exp(fresh_top - top_score)
        stale_weight = jnp.exp(stale_top - top_score)
        numer = fresh_acc * fresh_weight[..., None] + stale_acc * stale_weight[..., None]
        denom = fresh_sum * fresh_weight + stale_sum * stale_weight
        return (numer / denom[..., None]).astype(jnp.bfloat16)
    outputs = lax.map(per_head, (split_heads(projected[:, :, 0]), split_heads(projected[:, :, 1]), split_heads(projected[:, :, 2]), split_heads(stale_flat[:, :, 0]), split_heads(stale_flat[:, :, 1])))
    attended = outputs.transpose(1, 2, 0, 3).reshape(requests, row_count, column_count)
    mixed_rows = jnp.dot(attended.reshape(-1, column_count), weight_out, preferred_element_type=jnp.float32).reshape(requests, row_count, model_width)
    result = (token_rows.astype(jnp.float32) + gate_vec * mixed_rows).astype(jnp.bfloat16)
    key_value = projected[:, :, 1:]
    split_at = patches * capacity
    return (result[:, :split_at].reshape(video.shape), result[:, split_at:], key_value[:, :split_at].reshape(requests, patches, capacity, 2, column_count), key_value[:, split_at:])

def reference(video, text, patch_lengths, text_len, timestep, w_mod, w_qkv, w_out, stale_cache):
    layer_one = apply_layer(video, text, w_mod[0], w_qkv[0], w_out[0], stale_cache[0], patch_lengths, text_len, timestep)
    layer_two = apply_layer(layer_one[0], layer_one[1], w_mod[1], w_qkv[1], w_out[1], stale_cache[1], patch_lengths, text_len, timestep)
    return (jnp.stack([layer_one[0], layer_two[0]]), jnp.stack([layer_one[1], layer_two[1]]), jnp.stack([layer_one[2], layer_two[2]]), jnp.stack([layer_one[3], layer_two[3]]))
```

```python
import math

import jax
import jax.numpy as jnp
from jax import lax
from jax.experimental import pallas as pl
from jax.experimental.pallas import tpu as pltpu
from jax.sharding import PartitionSpec as P

HEAD = 64
LANES = 128
EPS = 1e-05
NEG = -1e30
VMEM_LIMIT = 56 * 1024 * 1024


def modulation(timestep, weight):
    half_width = weight.shape[0] // 2
    frequency = jnp.exp(-math.log(10000.0) * jnp.arange(half_width, dtype=jnp.float32) / half_width)
    phases = timestep.astype(jnp.float32)[0] * frequency
    embedding = jnp.concatenate([jnp.cos(phases), jnp.sin(phases)])
    active = jax.nn.silu(embedding).astype(jnp.bfloat16)
    return jnp.dot(active[None, :], weight, preferred_element_type=jnp.float32)


def swap(value, mapping):
    pairs = []
    for section in range(2):
        for part in range(4):
            target = mapping(section, part)
            if target is not None:
                pairs.append((section * 4 + part, target[0] * 4 + target[1]))
    return lax.ppermute(value, ("section", "mp"), pairs)


def swap_core(value):
    return swap(value, lambda section, part: (section, part ^ 1))


def swap_chip(value):
    return swap(value, lambda section, part: (section, part ^ 2))


def next_section(value):
    return swap(value, lambda section, part: (1, part ^ 2) if section == 0 else None)


def qkv_kernel(*refs, rows, units, stale_rows):
    if stale_rows:
        x_ref, mod_ref, w_ref, stale_ref, o_ref, normed_ref, w_buf, sems = refs
    else:
        x_ref, mod_ref, w_ref, o_ref, normed_ref, w_buf, sems = refs
    parts, width, columns = w_ref.shape
    chunks = sems.shape[1]
    depth = width // chunks
    copies = []
    for part in range(parts):
        for chunk in range(chunks):
            span = pl.ds(chunk * depth, depth)
            copy = pltpu.make_async_copy(
                w_ref.at[part, span, :], w_buf.at[part, span, :], sems.at[part, chunk]
            )
            copy.start()
            copies.append(copy)
    total = x_ref.shape[0]
    step = 16
    shift = mod_ref[0:1, :]
    scale = 1.0 + mod_ref[1:2, :]
    for start in range(0, total, step):
        values = x_ref[start : start + step, :].astype(jnp.float32)
        center = values - jnp.mean(values, axis=-1, keepdims=True)
        spread = jnp.mean(center * center, axis=-1, keepdims=True)
        normed = center * lax.rsqrt(spread + EPS) * scale + shift
        normed_ref[start : start + step, :] = normed.astype(jnp.bfloat16)
    blocks = columns // LANES
    if stale_rows:
        for unit in range(units):
            o_ref[unit, 3 * rows : 3 * rows + stale_rows, :] = stale_ref[unit]
    for unit in range(units, o_ref.shape[0]):
        o_ref[unit] = jnp.zeros(o_ref.shape[1:], o_ref.dtype)
    for part in range(parts):
        acc = jnp.zeros((total, columns), jnp.float32)
        for chunk in range(chunks):
            copies[part * chunks + chunk].wait()
            acc += jnp.dot(
                normed_ref[:, chunk * depth : (chunk + 1) * depth],
                w_buf[part, chunk * depth : (chunk + 1) * depth, :],
                preferred_element_type=jnp.float32,
            )
        for request in range(total // rows):
            for block in range(blocks):
                o_ref[request * blocks + block, part * rows : (part + 1) * rows, :] = acc[
                    request * rows : (request + 1) * rows, block * LANES : (block + 1) * LANES
                ].astype(jnp.bfloat16)


def qkv_call(x, mod, weight, stale, rows, devices):
    total, width = x.shape
    parts, _, columns = weight.shape
    units = (total // rows) * (columns // LANES)
    stale_rows = 0 if stale is None else stale.shape[1]
    chunks = 2
    vmem = pl.BlockSpec(memory_space=pltpu.VMEM)
    operands = [x, mod, weight] + ([] if stale is None else [stale])
    return pl.pallas_call(
        lambda *refs: qkv_kernel(*refs, rows=rows, units=units, stale_rows=stale_rows),
        out_shape=jax.ShapeDtypeStruct((devices, 3 * rows + stale_rows, LANES), jnp.bfloat16),
        in_specs=[vmem, vmem, pl.BlockSpec(memory_space=pl.ANY)] + [vmem] * (len(operands) - 3),
        out_specs=vmem,
        scratch_shapes=[
            pltpu.VMEM((total, width), jnp.bfloat16),
            pltpu.VMEM(weight.shape, jnp.bfloat16),
            pltpu.SemaphoreType.DMA((parts, chunks)),
        ],
        compiler_params=pltpu.CompilerParams(vmem_limit_bytes=VMEM_LIMIT),
        name="qkv",
    )(*operands)


def attention_kernel(lens_ref, recv_ref, stale_ref, o_ref, *, rows, per_dev, patches):
    devices = recv_ref.shape[0]
    capacity = devices * per_dev

    def block(ref, base, index):
        start = base + index * per_dev
        return ref[:, start : start + per_dev, :].reshape(capacity, LANES)

    groups = patches + 1
    fresh_k = [block(recv_ref, rows, index) for index in range(groups)]
    fresh_v = [block(recv_ref, 2 * rows, index) for index in range(groups)]
    stale_base = 3 * rows
    stale_k = [None] + [block(stale_ref, stale_base, index) for index in range(patches - 1)]
    stale_base += (patches - 1) * per_dev
    stale_v = [None] + [block(stale_ref, stale_base, index) for index in range(patches - 1)]
    slot = lax.broadcasted_iota(jnp.int32, (1, groups * capacity), 1)
    limit = jnp.zeros((1, groups * capacity), jnp.int32)
    for index in range(groups):
        limit = jnp.where(slot >= index * capacity, lens_ref[index] + index * capacity, limit)
    bias = jnp.where(slot < limit, 0.0, NEG)
    lane = lax.broadcasted_iota(jnp.int32, (1, LANES), 1)
    factor = HEAD ** (-0.5) * math.log2(math.e)
    for patch in range(patches):
        keys = jnp.concatenate(
            [fresh_k[i] if i <= patch else stale_k[i] for i in range(patches)] + [fresh_k[patches]], axis=0
        )
        values = jnp.concatenate(
            [fresh_v[i] if i <= patch else stale_v[i] for i in range(patches)] + [fresh_v[patches]], axis=0
        )
        for group in [patch, patches] if patch == 0 else [patch]:
            queries = block(recv_ref, 0, group)
            outs = []
            for head in range(2):
                mine = (lane < HEAD) if head == 0 else (lane >= HEAD)
                scores = lax.dot_general(
                    jnp.where(mine, queries, jnp.zeros_like(queries)),
                    keys,
                    (((1,), (1,)), ((), ())),
                    preferred_element_type=jnp.float32,
                )
                scores = scores + bias
                top = jnp.max(scores, axis=-1, keepdims=True)
                weights = jnp.exp2((scores - top) * factor)
                weight_sum = jnp.sum(weights, axis=-1, keepdims=True)
                acc = jnp.dot(
                    weights.astype(jnp.bfloat16), values, preferred_element_type=jnp.float32
                )
                outs.append(acc / weight_sum)
            out = jnp.where(lane < HEAD, outs[0], outs[1]).astype(jnp.bfloat16)
            start = group * per_dev
            o_ref[:, start : start + per_dev, :] = out.reshape(devices, per_dev, LANES)


def attention_call(lens, recv, stale, rows, per_dev, patches):
    devices = recv.shape[0]
    vmem = pl.BlockSpec(memory_space=pltpu.VMEM)
    return pl.pallas_call(
        lambda *refs: attention_kernel(*refs, rows=rows, per_dev=per_dev, patches=patches),
        out_shape=jax.ShapeDtypeStruct((devices, rows, LANES), jnp.bfloat16),
        in_specs=[pl.BlockSpec(memory_space=pltpu.SMEM), vmem, vmem],
        out_specs=vmem,
        compiler_params=pltpu.CompilerParams(vmem_limit_bytes=VMEM_LIMIT),
        name="attention",
    )(lens, recv, stale)


def out_kernel(recv_ref, gate_ref, w_ref, o_ref, mixed_ref, w_buf, sems, *, requests):
    depth, width = w_ref.shape
    rows = recv_ref.shape[1]
    blocks = depth // LANES
    chunks = sems.shape[0]
    span = width // chunks
    copies = []
    for chunk in range(chunks):
        at = pl.ds(chunk * span, span)
        copy = pltpu.make_async_copy(w_ref.at[:, at], w_buf.at[:, at], sems.at[chunk])
        copy.start()
        copies.append(copy)
    for request in range(requests):
        for block in range(blocks):
            mixed_ref[request * rows : (request + 1) * rows, block * LANES : (block + 1) * LANES] = recv_ref[
                request * blocks + block
            ]
    per_half = chunks // 2
    for chunk in range(chunks):
        copies[chunk].wait()
        acc = jnp.dot(
            mixed_ref[...],
            w_buf[:, chunk * span : (chunk + 1) * span],
            preferred_element_type=jnp.float32,
        )
        acc = acc * gate_ref[0:1, chunk * span : (chunk + 1) * span]
        at = (chunk % per_half) * span
        o_ref[chunk // per_half, :, at : at + span] = acc.astype(jnp.bfloat16)


def out_call(recv, gate, weight, requests):
    depth, width = weight.shape
    total = requests * recv.shape[1]
    chunks = 4
    vmem = pl.BlockSpec(memory_space=pltpu.VMEM)
    return pl.pallas_call(
        lambda *refs: out_kernel(*refs, requests=requests),
        out_shape=jax.ShapeDtypeStruct((2, total, width // 2), jnp.bfloat16),
        in_specs=[vmem, vmem, pl.BlockSpec(memory_space=pl.ANY)],
        out_specs=vmem,
        scratch_shapes=[
            pltpu.VMEM((total, depth), jnp.bfloat16),
            pltpu.VMEM(weight.shape, jnp.bfloat16),
            pltpu.SemaphoreType.DMA((chunks,)),
        ],
        compiler_params=pltpu.CompilerParams(vmem_limit_bytes=VMEM_LIMIT),
        name="out_projection",
    )(recv, gate, weight)


def body(video, text, patch_lengths, text_len, timestep, w_mod, w_qkv, w_out, stale_cache):
    section = lax.axis_index("section")
    core = lax.axis_index("mp") % 2
    chip = lax.axis_index("mp") // 2
    devices = lax.axis_size("seq")
    requests, patches, per_dev, width = video.shape
    text_dev = text.shape[1]
    columns = w_out.shape[1]
    blocks = columns // LANES
    units = requests * blocks
    rows = patches * per_dev + text_dev
    half = width // 2

    def in_order(mine, other, which):
        return jnp.where(which == 0, jnp.concatenate([mine, other], -1), jnp.concatenate([other, mine], -1))

    own_mod = modulation(timestep, w_mod[0])
    chip_mod = in_order(own_mod, swap_core(own_mod), core)
    modulated = in_order(chip_mod, swap_chip(chip_mod), chip).reshape(3, width)
    gate = modulated[2:3]

    weight_qkv = w_qkv[0].transpose(1, 0, 2)
    weight_out = w_out[0]
    stale = stale_cache[0][:, 1:].reshape(requests, (patches - 1) * per_dev, 2, blocks, LANES)
    stale = stale.transpose(0, 3, 2, 1, 4).reshape(units, 2 * (patches - 1) * per_dev, LANES)
    x = jnp.concatenate([video.reshape(requests, patches * per_dev, width), text], axis=1)
    x = x.reshape(requests * rows, width)

    request = jnp.minimum(lax.axis_index("seq") // blocks, requests - 1)
    lens = jnp.concatenate([patch_lengths, text_len[:, None]], axis=1)
    lens = lax.dynamic_index_in_dim(lens, request, 0, keepdims=False)

    def half_of(value):
        return lax.dynamic_slice_in_dim(value, core * half, half, 1)

    def after_qkv(x_now, sent, stale_recv):
        recv = lax.all_to_all(sent, "seq", 0, 0, tiled=True)
        attended = attention_call(
            lens, recv, recv if stale_recv is None else stale_recv, rows, per_dev, patches
        )
        mixed = lax.all_to_all(attended, "seq", 0, 0, tiled=True)
        partial = out_call(mixed, gate, weight_out, requests)
        mine = lax.dynamic_index_in_dim(partial, core, 0, keepdims=False)
        other = lax.dynamic_index_in_dim(partial, 1 - core, 0, keepdims=False)
        on_chip = (mine.astype(jnp.float32) + swap_core(other).astype(jnp.float32)).astype(jnp.bfloat16)
        summed = on_chip.astype(jnp.float32) + swap_chip(on_chip).astype(jnp.float32)
        result = (half_of(x_now).astype(jnp.float32) + summed).astype(jnp.bfloat16)
        return recv, result

    sent_0 = qkv_call(x, modulated, weight_qkv, stale, rows, devices)
    recv_0, result_0 = after_qkv(x, sent_0, None)
    arrived = next_section(result_0)
    x_1 = in_order(arrived, swap_core(arrived), core)
    sent_1 = qkv_call(x_1, modulated, weight_qkv, None, rows, devices)
    _, result_1 = after_qkv(x_1, sent_1, recv_0)

    result = jnp.where(section == 0, result_0, result_1)
    result = in_order(result, swap_core(result), core).reshape(requests, rows, width)
    key_value = jnp.where(section == 0, sent_0[:units, rows : 3 * rows], sent_1[:units, rows : 3 * rows])
    key_value = key_value.reshape(requests, blocks, 2, rows, LANES).transpose(0, 3, 2, 1, 4)
    key_value = key_value.reshape(requests, rows, 2, columns)
    split_at = patches * per_dev
    return (
        result[:, :split_at].reshape(1, requests, patches, per_dev, width),
        result[:, split_at:][None],
        key_value[:, :split_at].reshape(1, requests, patches, per_dev, 2, columns),
        key_value[:, split_at:][None],
    )


def solution(mesh):
    placed = (
        P(None, None, "seq", None),
        P(None, "seq", None),
        P(),
        P(),
        P(),
        P("section", None, "mp"),
        P("section", None, None, "mp"),
        P("section", "mp", None),
        P("section", None, None, "seq", None, "mp"),
    )
    return jax.shard_map(
        body,
        mesh=mesh,
        in_specs=placed,
        out_specs=(
            P("section", None, None, "seq", None),
            P("section", None, "seq", None),
            P("section", None, None, "seq", None, "mp"),
            P("section", None, "seq", None, "mp"),
        ),
        check_vma=False,
    )
```

```python
import math

import jax
import jax.numpy as jnp
from jax import lax
from jax.experimental import pallas as pl
from jax.experimental.pallas import tpu as pltpu
from jax.sharding import PartitionSpec as P

HEAD = 64
LANES = 128
EPS = 1e-05
NEG = -1e30
VMEM_LIMIT = 12 * 1024 * 1024


def modulation(timestep, weight):
    half_width = weight.shape[0] // 2
    frequency = jnp.exp(-math.log(10000.0) * jnp.arange(half_width, dtype=jnp.float32) / half_width)
    phases = timestep.astype(jnp.float32)[0] * frequency
    embedding = jnp.concatenate([jnp.cos(phases), jnp.sin(phases)])
    active = jax.nn.silu(embedding).astype(jnp.bfloat16)
    return jnp.dot(active[None, :], weight, preferred_element_type=jnp.float32)


def swap(value, mapping):
    pairs = []
    for section in range(2):
        for part in range(4):
            target = mapping(section, part)
            if target is not None:
                pairs.append((section * 4 + part, target[0] * 4 + target[1]))
    return lax.ppermute(value, ("section", "mp"), pairs)


def swap_core(value):
    return swap(value, lambda section, part: (section, part ^ 1))


def swap_chip(value):
    return swap(value, lambda section, part: (section, part ^ 2))


def next_section(value):
    return swap(value, lambda section, part: (1, part ^ 2) if section == 0 else None)

VMEM = pl.BlockSpec(memory_space=pltpu.VMEM)
SMEM = pl.BlockSpec(memory_space=pltpu.SMEM)
ANY = pl.BlockSpec(memory_space=pl.ANY)
PARAMS = pltpu.CompilerParams(vmem_limit_bytes=VMEM_LIMIT)


def centered(values):
    values = values.astype(jnp.float32)
    center = values - jnp.mean(values, axis=-1, keepdims=True)
    spread = jnp.mean(center * center, axis=-1, keepdims=True)
    return center * lax.rsqrt(spread + EPS)


def prepare_kernel(
    video_ref, text_ref, w_ref, stale_ref, half_ref, unit_ref, packed_ref, w_vmem, video_buf, text_buf, stale_buf, x_ref, sems
):
    requests, patches, per_dev, width = video_ref.shape
    first = [
        pltpu.make_async_copy(stale_ref, stale_buf, sems.at[0]),
        pltpu.make_async_copy(video_ref, video_buf, sems.at[1]),
        pltpu.make_async_copy(text_ref, text_buf, sems.at[2]),
    ]
    loads = [
        pltpu.make_async_copy(w_ref.at[part], w_vmem.at[part], sems.at[3 + part]) for part in range(w_ref.shape[0])
    ]
    for copy in first + loads:
        copy.start()
    first[0].wait()
    blocks = w_ref.shape[2] // LANES
    for request in range(requests):
        for patch in range(1, patches):
            both = stale_buf[request, patch]
            for kind in range(2):
                values = both[:, kind, :]
                row = (kind * (patches - 1) + patch - 1) * per_dev
                for block in range(blocks):
                    packed_ref[request * blocks + block, row : row + per_dev, :] = values[
                        :, block * LANES : (block + 1) * LANES
                    ]
    for copy in first[1:]:
        copy.wait()
    row = 0
    for request in range(requests):
        for patch in range(patches + 1):
            values = video_buf[request, patch] if patch < patches else text_buf[request]
            x_ref[row : row + per_dev, :] = values
            unit_ref[row : row + per_dev, :] = centered(values)
            row += per_dev
    half = width // 2
    core = lax.axis_index("mp") % 2
    half_ref[...] = x_ref[:, pl.ds(pl.multiple_of(core * half, LANES), half)]
    for copy in loads:
        copy.wait()


def prepare_call(video, text, weight, stale):
    requests, patches, per_dev, width = video.shape
    total = requests * (patches + 1) * per_dev
    units = requests * (weight.shape[2] // LANES)
    operands = [pltpu.with_memory_space_constraint(value, pltpu.HBM) for value in (video, text, weight, stale)]
    return pl.pallas_call(
        prepare_kernel,
        out_shape=(
            pltpu.VMEM((total, width // 2), jnp.bfloat16),
            pltpu.VMEM((total, width), jnp.float32),
            pltpu.VMEM((units, 2 * (patches - 1) * per_dev, LANES), jnp.bfloat16),
            pltpu.VMEM(weight.shape, jnp.bfloat16),
        ),
        in_specs=[ANY] * 4,
        out_specs=(VMEM,) * 4,
        scratch_shapes=[
            pltpu.VMEM(video.shape, jnp.bfloat16),
            pltpu.VMEM(text.shape, jnp.bfloat16),
            pltpu.VMEM(stale.shape, jnp.bfloat16),
            pltpu.VMEM((total, width), jnp.bfloat16),
            pltpu.SemaphoreType.DMA((3 + weight.shape[0],)),
        ],
        compiler_params=PARAMS,
        name="prepare",
    )(*operands)


def project(normed_ref, w_ref, o_ref, kv_ref, rows):
    parts, _, columns = w_ref.shape
    blocks = columns // LANES
    requests = normed_ref.shape[0] // rows
    for unit in range(requests * blocks, o_ref.shape[0]):
        o_ref[unit] = jnp.zeros(o_ref.shape[1:], o_ref.dtype)
    for part in range(parts):
        acc = jnp.dot(normed_ref[...], w_ref[part], preferred_element_type=jnp.float32)
        if part:
            kv_ref[part - 1] = acc.astype(jnp.bfloat16)
        for request in range(requests):
            for block in range(blocks):
                o_ref[request * blocks + block, part * rows : (part + 1) * rows, :] = acc[
                    request * rows : (request + 1) * rows, block * LANES : (block + 1) * LANES
                ].astype(jnp.bfloat16)


def first_kernel(
    unit_ref, mod_0, mod_1, mod_2, mod_3, w_ref, stale_ref, o_ref, kv_ref, mod_ref, pieces_ref, normed_ref, *, rows
):
    for index, piece in enumerate((mod_0, mod_1, mod_2, mod_3)):
        pieces_ref[lax.axis_index("mp") ^ index, 0:1, :] = piece[...]
    total, width = unit_ref.shape
    piece_width = mod_0.shape[1]
    for line in range(3):
        start = line * width
        while start < (line + 1) * width:
            slot, at = divmod(start, piece_width)
            count = min(piece_width - at, (line + 1) * width - start)
            to = start - line * width
            mod_ref[line : line + 1, to : to + count] = pieces_ref[slot, 0:1, at : at + count]
            start += count
    step = 16
    for start in range(0, total, step):
        normed = unit_ref[start : start + step, :] * (1.0 + mod_ref[1:2, :]) + mod_ref[0:1, :]
        normed_ref[start : start + step, :] = normed.astype(jnp.bfloat16)
    for unit in range(stale_ref.shape[0]):
        o_ref[unit, 3 * rows :, :] = stale_ref[unit]
    project(normed_ref, w_ref, o_ref, kv_ref, rows)


def first_call(unit, mods, weight, stale, rows, devices):
    total, width = unit.shape
    return pl.pallas_call(
        lambda *refs: first_kernel(*refs, rows=rows),
        out_shape=(
            jax.ShapeDtypeStruct((devices, 3 * rows + stale.shape[1], LANES), jnp.bfloat16),
            jax.ShapeDtypeStruct((2, total, weight.shape[2]), jnp.bfloat16),
            pltpu.VMEM((3, width), jnp.float32),
        ),
        in_specs=[VMEM] * 7,
        out_specs=(VMEM,) * 3,
        scratch_shapes=[
            pltpu.VMEM((4, 8, mods[0].shape[1]), jnp.float32),
            pltpu.VMEM((total, width), jnp.bfloat16),
        ],
        compiler_params=PARAMS,
        name="first_qkv",
    )(unit, *mods, weight, stale)


def second_kernel(mine_ref, other_ref, mod_ref, w_ref, o_ref, kv_ref, x_ref, normed_ref, *, rows):
    total, half = mine_ref.shape
    core = lax.axis_index("mp") % 2
    x_ref[:, pl.ds(pl.multiple_of(core * half, LANES), half)] = mine_ref[...]
    x_ref[:, pl.ds(pl.multiple_of((1 - core) * half, LANES), half)] = other_ref[...]
    step = 16
    for start in range(0, total, step):
        normed = centered(x_ref[start : start + step, :]) * (1.0 + mod_ref[1:2, :]) + mod_ref[0:1, :]
        normed_ref[start : start + step, :] = normed.astype(jnp.bfloat16)
    project(normed_ref, w_ref, o_ref, kv_ref, rows)


def second_call(mine, other, mod, weight, rows, devices):
    total, half = mine.shape
    return pl.pallas_call(
        lambda *refs: second_kernel(*refs, rows=rows),
        out_shape=(
            jax.ShapeDtypeStruct((devices, 3 * rows, LANES), jnp.bfloat16),
            jax.ShapeDtypeStruct((2, total, weight.shape[2]), jnp.bfloat16),
        ),
        in_specs=[VMEM] * 4,
        out_specs=(VMEM, VMEM),
        scratch_shapes=[pltpu.VMEM((total, 2 * half), jnp.bfloat16)] * 2,
        compiler_params=PARAMS,
        name="second_qkv",
    )(mine, other, mod, weight)


def attention_kernel(*refs, rows, per_dev, patches, blocks):
    if len(refs) == 8:
        lens_ref, text_ref, recv_ref, stale_ref, w_ref, o_ref, w_vmem, sem = refs
        copy = pltpu.make_async_copy(w_ref, w_vmem, sem)
        copy.start()
    else:
        lens_ref, text_ref, recv_ref, stale_ref, o_ref = refs
        copy = None
    devices = recv_ref.shape[0]
    capacity = devices * per_dev

    def block(ref, base, index):
        start = base + index * per_dev
        return ref[:, start : start + per_dev, :].reshape(capacity, LANES)

    groups = patches + 1
    fresh_k = [block(recv_ref, rows, index) for index in range(groups)]
    fresh_v = [block(recv_ref, 2 * rows, index) for index in range(groups)]
    stale_base = 3 * rows
    stale_k = [None] + [block(stale_ref, stale_base, index) for index in range(patches - 1)]
    stale_base += (patches - 1) * per_dev
    stale_v = [None] + [block(stale_ref, stale_base, index) for index in range(patches - 1)]
    slot = lax.broadcasted_iota(jnp.int32, (1, groups * capacity), 1)
    limit = jnp.zeros((1, groups * capacity), jnp.int32)
    request = jnp.minimum(lax.axis_index("seq") // blocks, lens_ref.shape[0] - 1)
    for index in range(groups):
        length = lens_ref[request, index] if index < patches else text_ref[request]
        limit = jnp.where(slot >= index * capacity, length + index * capacity, limit)
    bias = jnp.where(slot < limit, 0.0, NEG)
    lane = lax.broadcasted_iota(jnp.int32, (1, LANES), 1)
    factor = HEAD ** (-0.5) * math.log2(math.e)
    for patch in range(patches):
        keys = jnp.concatenate(
            [fresh_k[i] if i <= patch else stale_k[i] for i in range(patches)] + [fresh_k[patches]], axis=0
        )
        values = jnp.concatenate(
            [fresh_v[i] if i <= patch else stale_v[i] for i in range(patches)] + [fresh_v[patches]], axis=0
        )
        for group in [patch, patches] if patch == 0 else [patch]:
            queries = block(recv_ref, 0, group)
            outs = []
            for head in range(2):
                mine = (lane < HEAD) if head == 0 else (lane >= HEAD)
                scores = lax.dot_general(
                    jnp.where(mine, queries, jnp.zeros_like(queries)),
                    keys,
                    (((1,), (1,)), ((), ())),
                    preferred_element_type=jnp.float32,
                )
                scores = scores + bias
                top = jnp.max(scores, axis=-1, keepdims=True)
                weights = jnp.exp2((scores - top) * factor)
                weight_sum = jnp.sum(weights, axis=-1, keepdims=True)
                acc = jnp.dot(
                    weights.astype(jnp.bfloat16), values, preferred_element_type=jnp.float32
                )
                outs.append(acc / weight_sum)
            out = jnp.where(lane < HEAD, outs[0], outs[1]).astype(jnp.bfloat16)
            start = group * per_dev
            o_ref[:, start : start + per_dev, :] = out.reshape(devices, per_dev, LANES)
    if copy is not None:
        copy.wait()


def attention_call(lens, text_len, recv, stale, weight, rows, per_dev, blocks):
    devices = recv.shape[0]
    outs = jax.ShapeDtypeStruct((devices, rows, LANES), jnp.bfloat16)
    loads = weight is not None
    return pl.pallas_call(
        lambda *refs: attention_kernel(*refs, rows=rows, per_dev=per_dev, patches=lens.shape[1], blocks=blocks),
        out_shape=(outs, pltpu.VMEM(weight.shape, weight.dtype)) if loads else outs,
        in_specs=[SMEM, SMEM, VMEM, VMEM] + ([ANY] if loads else []),
        out_specs=(VMEM, VMEM) if loads else VMEM,
        scratch_shapes=[pltpu.SemaphoreType.DMA] if loads else [],
        compiler_params=PARAMS,
        name="attention",
    )(lens, text_len, recv, stale, *([pltpu.with_memory_space_constraint(weight, pltpu.HBM)] if loads else []))


def out_kernel(recv_ref, mod_ref, w_ref, other_ref, mine_ref, mixed_ref):
    depth, width = w_ref.shape
    rows = recv_ref.shape[1]
    blocks = depth // LANES
    for request in range(mixed_ref.shape[0] // rows):
        for block in range(blocks):
            mixed_ref[request * rows : (request + 1) * rows, block * LANES : (block + 1) * LANES] = recv_ref[
                request * blocks + block
            ]
    half = width // 2
    core = lax.axis_index("mp") % 2
    for ref, index in ((other_ref, 1 - core), (mine_ref, core)):
        at = pl.ds(pl.multiple_of(index * half, LANES), half)
        acc = jnp.dot(mixed_ref[...], w_ref[:, at], preferred_element_type=jnp.float32)
        ref[...] = (acc * mod_ref[2:3, at]).astype(ref.dtype)


def out_call(recv, mod, weight, requests):
    depth, width = weight.shape
    total = requests * recv.shape[1]
    return pl.pallas_call(
        out_kernel,
        out_shape=(
            pltpu.VMEM((total, width // 2), jnp.bfloat16),
            pltpu.VMEM((total, width // 2), jnp.float32),
        ),
        in_specs=[VMEM, VMEM, VMEM],
        out_specs=(VMEM, VMEM),
        scratch_shapes=[pltpu.VMEM((total, depth), jnp.bfloat16)],
        compiler_params=PARAMS,
        name="out_projection",
    )(recv, mod, weight)


def store_kernel(mine_ref, other_ref, video_ref, text_ref, sems):
    _, requests, patches, per_dev, _ = video_ref.shape
    half = mine_ref.shape[1]
    core = lax.axis_index("mp") % 2
    copies = []
    for side, (source, index) in enumerate(((mine_ref, core), (other_ref, 1 - core))):
        at = pl.ds(pl.multiple_of(index * half, LANES), half)
        row = 0
        for request in range(requests):
            for patch in range(patches + 1):
                target = (
                    video_ref.at[0, request, patch, :, at]
                    if patch < patches
                    else text_ref.at[0, request, :, at]
                )
                copy = pltpu.make_async_copy(
                    source.at[pl.ds(row, per_dev), :], target, sems.at[side, row // per_dev]
                )
                copy.start()
                copies.append(copy)
                row += per_dev
    for copy in copies:
        copy.wait()


def store_call(mine, other, video_shape, text_shape):
    return pl.pallas_call(
        store_kernel,
        out_shape=(
            jax.ShapeDtypeStruct(video_shape, jnp.bfloat16),
            jax.ShapeDtypeStruct(text_shape, jnp.bfloat16),
        ),
        in_specs=[VMEM, VMEM],
        out_specs=(ANY, ANY),
        scratch_shapes=[pltpu.SemaphoreType.DMA((2, mine.shape[0] // video_shape[3]))],
        compiler_params=PARAMS,
        name="store",
    )(mine, other)


def body(video, text, patch_lengths, text_len, timestep, w_mod, w_qkv, w_out, stale_cache):
    devices = lax.axis_size("seq")
    requests, patches, per_dev, _ = video.shape
    columns = w_out.shape[1]
    blocks = columns // LANES
    rows = patches * per_dev + text.shape[1]

    timestep, is_first = lax.optimization_barrier((timestep, lax.axis_index("section") == 0))
    own_mod = modulation(timestep, w_mod[0])
    mods = [own_mod] + [
        swap(own_mod, lambda section, part, flip=flip: (section, part ^ flip)) for flip in (1, 2, 3)
    ]
    x_half, unit, stale, weight_qkv = prepare_call(video, text, w_qkv[0].transpose(1, 0, 2), stale_cache[0])

    def reduced(mixed, weight_out, mod):
        other, mine = out_call(mixed, mod, weight_out, requests)
        return (mine + swap_core(other).astype(jnp.float32)).astype(jnp.bfloat16)

    def added(x_half, on_chip, arrived):
        total = x_half.astype(jnp.float32) + (on_chip.astype(jnp.float32) + arrived.astype(jnp.float32))
        return total.astype(jnp.bfloat16)

    sent_0, kv_0, mod = first_call(unit, mods, weight_qkv, stale, rows, devices)
    recv_0 = lax.all_to_all(sent_0, "seq", 0, 0, tiled=True)
    attended, weight_out = attention_call(
        patch_lengths, text_len, recv_0, recv_0, w_out[0], rows, per_dev, blocks
    )
    on_chip = reduced(lax.all_to_all(attended, "seq", 0, 0, tiled=True), weight_out, mod)
    result_0 = added(x_half, on_chip, swap_chip(on_chip))

    x_half = next_section(result_0)
    sent_1, kv_1 = second_call(x_half, swap_core(x_half), mod, weight_qkv, rows, devices)
    recv_1 = lax.all_to_all(sent_1, "seq", 0, 0, tiled=True)
    attended = attention_call(patch_lengths, text_len, recv_1, recv_0, None, rows, per_dev, blocks)
    on_chip = reduced(lax.all_to_all(attended, "seq", 0, 0, tiled=True), weight_out, mod)
    arrived = swap_chip(on_chip)

    key_value = jnp.where(is_first, kv_0, kv_1).reshape(2, requests, rows, columns).transpose(1, 2, 0, 3)
    split_at = patches * per_dev
    cache_video = key_value[:, :split_at].reshape(1, requests, patches, per_dev, 2, columns)
    cache_text = key_value[:, split_at:][None]
    arrived, cache_video, cache_text = lax.optimization_barrier((arrived, cache_video, cache_text))

    result = jnp.where(is_first, result_0, added(x_half, on_chip, arrived))
    hidden_video, hidden_text = store_call(result, swap_core(result), (1,) + video.shape, (1,) + text.shape)
    return (hidden_video, hidden_text, cache_video, cache_text)


def solution(mesh):
    placed = (
        P(None, None, "seq", None),
        P(None, "seq", None),
        P(),
        P(),
        P(),
        P("section", None, "mp"),
        P("section", None, None, "mp"),
        P("section", "mp", None),
        P("section", None, None, "seq", None, "mp"),
    )
    return jax.shard_map(
        body,
        mesh=mesh,
        in_specs=placed,
        out_specs=(
            P("section", None, None, "seq", None),
            P("section", None, "seq", None),
            P("section", None, None, "seq", None, "mp"),
            P("section", None, "seq", None, "mp"),
        ),
        check_vma=False,
    )
```

```python
import math

import jax
import jax.numpy as jnp
from jax import lax
from jax.experimental import pallas as pl
from jax.experimental.pallas import tpu as pltpu
from jax.sharding import PartitionSpec as P

HEAD = 64
LANES = 128
EPS = 1e-05
NEG = -1e30
CHUNKS = 2
VMEM_LIMIT = 12 * 1024 * 1024


def modulation(timestep, weight):
    half_width = weight.shape[0] // 2
    frequency = jnp.exp(-math.log(10000.0) * jnp.arange(half_width, dtype=jnp.float32) / half_width)
    phases = timestep.astype(jnp.float32)[0] * frequency
    embedding = jnp.concatenate([jnp.cos(phases), jnp.sin(phases)])
    active = jax.nn.silu(embedding).astype(jnp.bfloat16)
    return jnp.dot(active[None, :], weight, preferred_element_type=jnp.float32)


def swap(value, mapping):
    pairs = []
    for section in range(2):
        for part in range(4):
            target = mapping(section, part)
            pairs.append((section * 4 + part, target[0] * 4 + target[1]))
    return lax.ppermute(value, ("section", "mp"), pairs)


def swap_core(value):
    return swap(value, lambda section, part: (section, part ^ 1))


def swap_chip(value):
    return swap(value, lambda section, part: (section, part ^ 2))


def next_section(value):
    return swap(value, lambda section, part: (1 - section, part ^ 2))

VMEM = pl.BlockSpec(memory_space=pltpu.VMEM)
SMEM = pl.BlockSpec(memory_space=pltpu.SMEM)
ANY = pl.BlockSpec(memory_space=pl.ANY)
PARAMS = pltpu.CompilerParams(vmem_limit_bytes=VMEM_LIMIT)


def centered(values):
    values = values.astype(jnp.float32)
    center = values - jnp.mean(values, axis=-1, keepdims=True)
    spread = jnp.mean(center * center, axis=-1, keepdims=True)
    return center * lax.rsqrt(spread + EPS)


def prepare_kernel(
    video_ref, text_ref, w_ref, stale_ref, unit_ref, packed_ref, w_vmem, *refs
):
    *half_refs, video_buf, text_buf, stale_buf, x_ref, sems = refs
    requests, patches, per_dev, width = video_ref.shape
    first = [
        pltpu.make_async_copy(stale_ref, stale_buf, sems.at[0]),
        pltpu.make_async_copy(video_ref, video_buf, sems.at[1]),
        pltpu.make_async_copy(text_ref, text_buf, sems.at[2]),
    ]
    load = pltpu.make_async_copy(w_ref.at[pl.ds(0, 2)], w_vmem, sems.at[3])
    for copy in first + [load]:
        copy.start()
    first[0].wait()
    blocks = w_ref.shape[2] // LANES
    for request in range(requests):
        for patch in range(1, patches):
            both = stale_buf[request, patch]
            for kind in range(2):
                values = both[:, kind, :]
                row = (kind * (patches - 1) + patch - 1) * per_dev
                for block in range(blocks):
                    packed_ref[request * blocks + block, row : row + per_dev, :] = values[
                        :, block * LANES : (block + 1) * LANES
                    ]
    for copy in first[1:]:
        copy.wait()
    row = 0
    for request in range(requests):
        for patch in range(patches + 1):
            values = video_buf[request, patch] if patch < patches else text_buf[request]
            x_ref[row : row + per_dev, :] = values
            unit_ref[row : row + per_dev, :] = centered(values)
            row += per_dev
    half = width // 2
    core = lax.axis_index("mp") % 2
    span = half // len(half_refs)
    for chunk, ref in enumerate(half_refs):
        ref[...] = x_ref[:, pl.ds(pl.multiple_of(core * half + chunk * span, LANES), span)]
    load.wait()


def prepare_call(video, text, weight, stale):
    requests, patches, per_dev, width = video.shape
    total = requests * (patches + 1) * per_dev
    units = requests * (weight.shape[2] // LANES)
    operands = [pltpu.with_memory_space_constraint(value, pltpu.HBM) for value in (video, text, weight, stale)]
    return pl.pallas_call(
        prepare_kernel,
        out_shape=(
            pltpu.VMEM((total, width), jnp.float32),
            pltpu.VMEM((units, 2 * (patches - 1) * per_dev, LANES), jnp.bfloat16),
            pltpu.VMEM((2,) + weight.shape[1:], jnp.bfloat16),
        )
        + (pltpu.VMEM((total, width // 2 // CHUNKS), jnp.bfloat16),) * CHUNKS,
        in_specs=[ANY] * 4,
        out_specs=(VMEM,) * (3 + CHUNKS),
        scratch_shapes=[
            pltpu.VMEM(video.shape, jnp.bfloat16),
            pltpu.VMEM(text.shape, jnp.bfloat16),
            pltpu.VMEM(stale.shape, jnp.bfloat16),
            pltpu.VMEM((total, width), jnp.bfloat16),
            pltpu.SemaphoreType.DMA((4,)),
        ],
        compiler_params=PARAMS,
        name="prepare",
    )(*operands)


def project(normed_ref, wqk_ref, wv_ref, o_ref, kv_ref, rows, load=None):
    columns = wv_ref.shape[1]
    blocks = columns // LANES
    requests = normed_ref.shape[0] // rows
    for unit in range(requests * blocks, o_ref.shape[0]):
        o_ref[unit] = jnp.zeros(o_ref.shape[1:], o_ref.dtype)
    for part in range(3):
        if part == 2 and load is not None:
            load.wait()
        weight = wqk_ref[part] if part < 2 else wv_ref[...]
        acc = jnp.dot(normed_ref[...], weight, preferred_element_type=jnp.float32)
        if part:
            kv_ref[part - 1] = acc.astype(jnp.bfloat16)
        for request in range(requests):
            for block in range(blocks):
                o_ref[request * blocks + block, part * rows : (part + 1) * rows, :] = acc[
                    request * rows : (request + 1) * rows, block * LANES : (block + 1) * LANES
                ].astype(jnp.bfloat16)


def first_kernel(
    unit_ref,
    mod_0,
    mod_1,
    mod_2,
    mod_3,
    wqk_ref,
    w_ref,
    stale_ref,
    o_ref,
    kv_ref,
    mod_ref,
    wv_ref,
    pieces_ref,
    normed_ref,
    sem,
    *,
    rows,
):
    load = pltpu.make_async_copy(w_ref.at[2], wv_ref, sem)
    load.start()
    for index, piece in enumerate((mod_0, mod_1, mod_2, mod_3)):
        pieces_ref[lax.axis_index("mp") ^ index, 0:1, :] = piece[...]
    total, width = unit_ref.shape
    piece_width = mod_0.shape[1]
    for line in range(3):
        start = line * width
        while start < (line + 1) * width:
            slot, at = divmod(start, piece_width)
            count = min(piece_width - at, (line + 1) * width - start)
            to = start - line * width
            mod_ref[line : line + 1, to : to + count] = pieces_ref[slot, 0:1, at : at + count]
            start += count
    step = 16
    for start in range(0, total, step):
        normed = unit_ref[start : start + step, :] * (1.0 + mod_ref[1:2, :]) + mod_ref[0:1, :]
        normed_ref[start : start + step, :] = normed.astype(jnp.bfloat16)
    for unit in range(stale_ref.shape[0]):
        o_ref[unit, 3 * rows :, :] = stale_ref[unit]
    project(normed_ref, wqk_ref, wv_ref, o_ref, kv_ref, rows, load)


def first_call(unit, mods, weight_qk, weight, stale, rows, devices):
    total, width = unit.shape
    return pl.pallas_call(
        lambda *refs: first_kernel(*refs, rows=rows),
        out_shape=(
            jax.ShapeDtypeStruct((devices, 3 * rows + stale.shape[1], LANES), jnp.bfloat16),
            jax.ShapeDtypeStruct((2, total, weight.shape[2]), jnp.bfloat16),
            pltpu.VMEM((3, width), jnp.float32),
            pltpu.VMEM(weight.shape[1:], jnp.bfloat16),
        ),
        in_specs=[VMEM] * 6 + [ANY, VMEM],
        out_specs=(VMEM,) * 4,
        scratch_shapes=[
            pltpu.VMEM((4, 8, mods[0].shape[1]), jnp.float32),
            pltpu.VMEM((total, width), jnp.bfloat16),
            pltpu.SemaphoreType.DMA,
        ],
        compiler_params=PARAMS,
        name="first_qkv",
    )(unit, *mods, weight_qk, pltpu.with_memory_space_constraint(weight, pltpu.HBM), stale)


def second_kernel(
    mod_ref, wqk_ref, wv_ref, kv_0_ref, *refs, rows
):
    mine_refs, other_refs, before_refs = (refs[i * CHUNKS : (i + 1) * CHUNKS] for i in range(3))
    o_ref, kv_ref, *base_refs, x_ref, normed_ref = refs[3 * CHUNKS :]
    total, span = mine_refs[0].shape
    half = span * CHUNKS
    core = lax.axis_index("mp") % 2
    for chunk in range(CHUNKS):
        x_ref[:, pl.ds(pl.multiple_of(core * half + chunk * span, LANES), span)] = mine_refs[chunk][...]
        x_ref[:, pl.ds(pl.multiple_of((1 - core) * half + chunk * span, LANES), span)] = other_refs[chunk][...]
    step = 16
    for start in range(0, total, step):
        normed = centered(x_ref[start : start + step, :]) * (1.0 + mod_ref[1:2, :]) + mod_ref[0:1, :]
        normed_ref[start : start + step, :] = normed.astype(jnp.bfloat16)
    project(normed_ref, wqk_ref, wv_ref, o_ref, kv_ref, rows)
    is_first = lax.axis_index("section") == 0

    @pl.when(is_first)
    def _():
        kv_ref[...] = kv_0_ref[...]
        for base_ref, before_ref in zip(base_refs, before_refs):
            base_ref[...] = before_ref[...]

    @pl.when(jnp.logical_not(is_first))
    def _():
        for base_ref, mine_ref in zip(base_refs, mine_refs):
            base_ref[...] = mine_ref[...]


def second_call(mine, other, before, kv_0, mod, weight_qk, weight_v, rows, devices):
    total, span = mine[0].shape
    return pl.pallas_call(
        lambda *refs: second_kernel(*refs, rows=rows),
        out_shape=(
            jax.ShapeDtypeStruct((devices, 3 * rows, LANES), jnp.bfloat16),
            jax.ShapeDtypeStruct(kv_0.shape, jnp.bfloat16),
        )
        + (pltpu.VMEM((total, span), jnp.bfloat16),) * CHUNKS,
        in_specs=[VMEM] * (4 + 3 * CHUNKS),
        out_specs=(VMEM,) * (2 + CHUNKS),
        scratch_shapes=[pltpu.VMEM((total, 2 * CHUNKS * span), jnp.bfloat16)] * 2,
        compiler_params=PARAMS,
        name="second_qkv",
    )(mod, weight_qk, weight_v, kv_0, *mine, *other, *before)


def attention_kernel(*refs, rows, per_dev, patches, blocks):
    if len(refs) == 8:
        lens_ref, text_ref, recv_ref, stale_ref, w_ref, o_ref, w_vmem, sem = refs
        copy = pltpu.make_async_copy(w_ref, w_vmem, sem)
        copy.start()
    else:
        lens_ref, text_ref, recv_ref, stale_ref, o_ref = refs
        copy = None
    devices = recv_ref.shape[0]
    capacity = devices * per_dev

    def block(ref, base, index):
        start = base + index * per_dev
        return ref[:, start : start + per_dev, :].reshape(capacity, LANES)

    groups = patches + 1
    fresh_k = [block(recv_ref, rows, index) for index in range(groups)]
    fresh_v = [block(recv_ref, 2 * rows, index) for index in range(groups)]
    stale_base = 3 * rows
    stale_k = [None] + [block(stale_ref, stale_base, index) for index in range(patches - 1)]
    stale_base += (patches - 1) * per_dev
    stale_v = [None] + [block(stale_ref, stale_base, index) for index in range(patches - 1)]
    slot = lax.broadcasted_iota(jnp.int32, (1, groups * capacity), 1)
    limit = jnp.zeros((1, groups * capacity), jnp.int32)
    request = jnp.minimum(lax.axis_index("seq") // blocks, lens_ref.shape[0] - 1)
    for index in range(groups):
        length = lens_ref[request, index] if index < patches else text_ref[request]
        limit = jnp.where(slot >= index * capacity, length + index * capacity, limit)
    bias = jnp.where(slot < limit, 0.0, NEG)
    lane = lax.broadcasted_iota(jnp.int32, (1, LANES), 1)
    ones = jnp.ones((groups * capacity, LANES), jnp.bfloat16)
    factor = HEAD ** (-0.5) * math.log2(math.e)
    for patch in range(patches):
        keys = jnp.concatenate(
            [fresh_k[i] if i <= patch else stale_k[i] for i in range(patches)] + [fresh_k[patches]], axis=0
        )
        values = jnp.concatenate(
            [fresh_v[i] if i <= patch else stale_v[i] for i in range(patches)] + [fresh_v[patches]], axis=0
        )
        members = [patch, patches] if patch == 0 else [patch]
        queries = [block(recv_ref, 0, group) for group in members]
        queries = [jnp.where(lane < HEAD, q, jnp.zeros_like(q)) for q in queries] + [
            jnp.where(lane < HEAD, jnp.zeros_like(q), q) for q in queries
        ]
        scores = lax.dot_general(
            jnp.concatenate(queries, axis=0),
            keys,
            (((1,), (1,)), ((), ())),
            preferred_element_type=jnp.float32,
        )
        scores = scores + bias
        top = jnp.max(scores, axis=-1, keepdims=True)
        weights = jnp.exp2((scores - top) * factor).astype(jnp.bfloat16)
        acc = jnp.dot(weights, jnp.concatenate([values, ones], axis=1), preferred_element_type=jnp.float32)
        acc = acc[:, :LANES] / acc[:, LANES:]
        for index, group in enumerate(members):
            lower = acc[index * capacity : (index + 1) * capacity]
            upper = acc[(len(members) + index) * capacity : (len(members) + index + 1) * capacity]
            out = jnp.where(lane < HEAD, lower, upper).astype(jnp.bfloat16)
            start = group * per_dev
            o_ref[:, start : start + per_dev, :] = out.reshape(devices, per_dev, LANES)
    if copy is not None:
        copy.wait()


def attention_call(lens, text_len, recv, stale, weight, rows, per_dev, blocks):
    devices = recv.shape[0]
    outs = jax.ShapeDtypeStruct((devices, rows, LANES), jnp.bfloat16)
    loads = weight is not None
    return pl.pallas_call(
        lambda *refs: attention_kernel(*refs, rows=rows, per_dev=per_dev, patches=lens.shape[1], blocks=blocks),
        out_shape=(outs, pltpu.VMEM(weight.shape, weight.dtype)) if loads else outs,
        in_specs=[SMEM, SMEM, VMEM, VMEM] + ([ANY] if loads else []),
        out_specs=(VMEM, VMEM) if loads else VMEM,
        scratch_shapes=[pltpu.SemaphoreType.DMA] if loads else [],
        compiler_params=PARAMS,
        name="attention",
    )(lens, text_len, recv, stale, *([pltpu.with_memory_space_constraint(weight, pltpu.HBM)] if loads else []))


def out_kernel(recv_ref, mod_ref, w_ref, *refs, last):
    *refs, mixed_ref = refs
    other_refs, mine_refs = refs[: len(refs) // 2], refs[len(refs) // 2 :]
    depth, width = w_ref.shape
    rows = recv_ref.shape[1]
    blocks = depth // LANES
    for request in range(mixed_ref.shape[0] // rows):
        for block in range(blocks):
            mixed_ref[request * rows : (request + 1) * rows, block * LANES : (block + 1) * LANES] = recv_ref[
                request * blocks + block
            ]
    half = width // 2
    span = half // len(other_refs)
    core = lax.axis_index("mp") % 2
    for refs, index in ((other_refs, 1 - core), (mine_refs, core)):
        for chunk, ref in enumerate(refs):
            at = pl.ds(pl.multiple_of(index * half + chunk * span, LANES), span)
            acc = jnp.dot(mixed_ref[...], w_ref[:, at], preferred_element_type=jnp.float32)
            acc = acc * mod_ref[2:3, at]
            if last:
                acc = jnp.where(lax.axis_index("section") == 0, jnp.zeros_like(acc), acc)
            ref[...] = acc.astype(ref.dtype)


def out_call(recv, mod, weight, requests, last):
    depth, width = weight.shape
    total = requests * recv.shape[1]
    return pl.pallas_call(
        lambda *refs: out_kernel(*refs, last=last),
        out_shape=[
            pltpu.VMEM((total, width // 2 // CHUNKS), dtype)
            for dtype in (jnp.bfloat16, jnp.float32)
            for _ in range(CHUNKS)
        ],
        in_specs=[VMEM, VMEM, VMEM],
        out_specs=[VMEM] * (2 * CHUNKS),
        scratch_shapes=[pltpu.VMEM((total, depth), jnp.bfloat16)],
        compiler_params=PARAMS,
        name="out_projection",
    )(recv, mod, weight)


def store_kernel(*refs):
    *pieces, video_ref, text_ref, sems = refs
    _, requests, patches, per_dev, _ = video_ref.shape
    span = pieces[0].shape[1]
    half = span * CHUNKS
    core = lax.axis_index("mp") % 2
    copies = []
    for side, source in enumerate(pieces):
        index = core if side < CHUNKS else 1 - core
        at = pl.ds(pl.multiple_of(index * half + side % CHUNKS * span, LANES), span)
        row = 0
        for request in range(requests):
            for patch in range(patches + 1):
                target = (
                    video_ref.at[0, request, patch, :, at]
                    if patch < patches
                    else text_ref.at[0, request, :, at]
                )
                copy = pltpu.make_async_copy(
                    source.at[pl.ds(row, per_dev), :], target, sems.at[side, row // per_dev]
                )
                copy.start()
                copies.append(copy)
                row += per_dev
    for copy in copies:
        copy.wait()


def store_call(mine, other, video_shape, text_shape):
    return pl.pallas_call(
        store_kernel,
        out_shape=(
            jax.ShapeDtypeStruct(video_shape, jnp.bfloat16),
            jax.ShapeDtypeStruct(text_shape, jnp.bfloat16),
        ),
        in_specs=[VMEM] * (2 * CHUNKS),
        out_specs=(ANY, ANY),
        scratch_shapes=[pltpu.SemaphoreType.DMA((2 * CHUNKS, mine[0].shape[0] // video_shape[3]))],
        compiler_params=PARAMS,
        name="store",
    )(*mine, *other)


def body(video, text, patch_lengths, text_len, timestep, w_mod, w_qkv, w_out, stale_cache):
    devices = lax.axis_size("seq")
    requests, patches, per_dev, _ = video.shape
    columns = w_out.shape[1]
    blocks = columns // LANES
    rows = patches * per_dev + text.shape[1]

    own_mod = modulation(timestep, w_mod[0])
    mods = [own_mod] + [
        swap(own_mod, lambda section, part, flip=flip: (section, part ^ flip)) for flip in (1, 2, 3)
    ]
    weight = w_qkv[0].transpose(1, 0, 2)
    unit, stale, weight_qk, *x_half = prepare_call(video, text, weight, stale_cache[0])

    def reduced(mixed, weight_out, mod, last):
        pieces = out_call(mixed, mod, weight_out, requests, last)
        return [
            (mine + swap_core(other).astype(jnp.float32)).astype(jnp.bfloat16)
            for other, mine in zip(pieces[:CHUNKS], pieces[CHUNKS:])
        ]

    def added(x_half, on_chip, arrived):
        return [
            (a.astype(jnp.float32) + (b.astype(jnp.float32) + c.astype(jnp.float32))).astype(jnp.bfloat16)
            for a, b, c in zip(x_half, on_chip, arrived)
        ]

    def each(function, values):
        return [function(value) for value in values]

    sent_0, kv_0, mod, weight_v = first_call(unit, mods, weight_qk, weight, stale, rows, devices)
    recv_0 = lax.all_to_all(sent_0, "seq", 0, 0, tiled=True)
    weight_out = w_out[0]
    attended = attention_call(patch_lengths, text_len, recv_0, recv_0, None, rows, per_dev, blocks)
    on_chip = reduced(lax.all_to_all(attended, "seq", 0, 0, tiled=True), weight_out, mod, False)
    result_0 = added(x_half, on_chip, each(swap_chip, on_chip))

    x_half = each(next_section, result_0)
    sent_1, key_value, *base = second_call(
        x_half, each(swap_core, x_half), result_0, kv_0, mod, weight_qk, weight_v, rows, devices
    )
    recv_1 = lax.all_to_all(sent_1, "seq", 0, 0, tiled=True)
    attended = attention_call(patch_lengths, text_len, recv_1, recv_0, None, rows, per_dev, blocks)
    on_chip = reduced(lax.all_to_all(attended, "seq", 0, 0, tiled=True), weight_out, mod, True)
    arrived = each(swap_chip, on_chip)

    key_value = key_value.reshape(2, requests, rows, columns).transpose(1, 2, 0, 3)
    split_at = patches * per_dev
    cache_video = key_value[:, :split_at].reshape(1, requests, patches, per_dev, 2, columns)
    cache_text = key_value[:, split_at:][None]
    arrived, cache_video, cache_text = lax.optimization_barrier((arrived, cache_video, cache_text))

    result = added(base, on_chip, arrived)
    hidden_video, hidden_text = store_call(result, each(swap_core, result), (1,) + video.shape, (1,) + text.shape)
    return (hidden_video, hidden_text, cache_video, cache_text)


def solution(mesh):
    placed = (
        P(None, None, "seq", None),
        P(None, "seq", None),
        P(),
        P(),
        P(),
        P("section", None, "mp"),
        P("section", None, None, "mp"),
        P("section", "mp", None),
        P("section", None, None, "seq", None, "mp"),
    )
    return jax.shard_map(
        body,
        mesh=mesh,
        in_specs=placed,
        out_specs=(
            P("section", None, None, "seq", None),
            P("section", None, "seq", None),
            P("section", None, None, "seq", None, "mp"),
            P("section", None, "seq", None, "mp"),
        ),
        check_vma=False,
    )
```

```python
import math

import jax
import jax.numpy as jnp
from jax import lax
from jax.experimental import pallas as pl
from jax.experimental.pallas import tpu as pltpu
from jax.sharding import PartitionSpec as P

HEAD = 64
LANES = 128
EPS = 1e-05
NEG = -1e30
CHUNKS = 2
VMEM_LIMIT = 12 * 1024 * 1024


def modulation(timestep, weight):
    half_width = weight.shape[0] // 2
    frequency = jnp.exp(-math.log(10000.0) * jnp.arange(half_width, dtype=jnp.float32) / half_width)
    phases = timestep.astype(jnp.float32)[0] * frequency
    embedding = jnp.concatenate([jnp.cos(phases), jnp.sin(phases)])
    active = jax.nn.silu(embedding).astype(jnp.bfloat16)
    return jnp.dot(active[None, :], weight, preferred_element_type=jnp.float32)


def swap(value, mapping):
    pairs = []
    for section in range(2):
        for part in range(4):
            target = mapping(section, part)
            pairs.append((section * 4 + part, target[0] * 4 + target[1]))
    return lax.ppermute(value, ("section", "mp"), pairs)


def swap_core(value):
    return swap(value, lambda section, part: (section, part ^ 1))


def swap_chip(value):
    return swap(value, lambda section, part: (section, part ^ 2))


def next_section(value):
    return swap(value, lambda section, part: (1 - section, part ^ 2))

VMEM = pl.BlockSpec(memory_space=pltpu.VMEM)
SMEM = pl.BlockSpec(memory_space=pltpu.SMEM)
ANY = pl.BlockSpec(memory_space=pl.ANY)
PARAMS = pltpu.CompilerParams(vmem_limit_bytes=VMEM_LIMIT)


def centered(values):
    values = values.astype(jnp.float32)
    center = values - jnp.mean(values, axis=-1, keepdims=True)
    spread = jnp.mean(center * center, axis=-1, keepdims=True)
    return center * lax.rsqrt(spread + EPS)


def prepare_kernel(
    video_ref, text_ref, w_ref, stale_ref, unit_ref, packed_ref, w_vmem, *refs
):
    *half_refs, video_buf, text_buf, stale_buf, x_ref, sems = refs
    requests, patches, per_dev, width = video_ref.shape
    first = [
        pltpu.make_async_copy(stale_ref, stale_buf, sems.at[0]),
        pltpu.make_async_copy(video_ref, video_buf, sems.at[1]),
        pltpu.make_async_copy(text_ref, text_buf, sems.at[2]),
    ]
    load = pltpu.make_async_copy(w_ref.at[pl.ds(0, 2)], w_vmem, sems.at[3])
    for copy in first + [load]:
        copy.start()
    first[0].wait()
    blocks = w_ref.shape[2] // LANES
    for request in range(requests):
        for patch in range(1, patches):
            both = stale_buf[request, patch]
            for kind in range(2):
                values = both[:, kind, :]
                row = (kind * (patches - 1) + patch - 1) * per_dev
                for block in range(blocks):
                    packed_ref[request * blocks + block, row : row + per_dev, :] = values[
                        :, block * LANES : (block + 1) * LANES
                    ]
    for copy in first[1:]:
        copy.wait()
    row = 0
    for request in range(requests):
        for patch in range(patches + 1):
            values = video_buf[request, patch] if patch < patches else text_buf[request]
            x_ref[row : row + per_dev, :] = values
            unit_ref[row : row + per_dev, :] = centered(values)
            row += per_dev
    half = width // 2
    core = lax.axis_index("mp") % 2
    span = half // len(half_refs)
    for chunk, ref in enumerate(half_refs):
        ref[...] = x_ref[:, pl.ds(pl.multiple_of(core * half + chunk * span, LANES), span)]
    load.wait()


def prepare_call(video, text, weight, stale):
    requests, patches, per_dev, width = video.shape
    total = requests * (patches + 1) * per_dev
    units = requests * (weight.shape[2] // LANES)
    operands = [pltpu.with_memory_space_constraint(value, pltpu.HBM) for value in (video, text, weight, stale)]
    return pl.pallas_call(
        prepare_kernel,
        out_shape=(
            pltpu.VMEM((total, width), jnp.float32),
            pltpu.VMEM((units, 2 * (patches - 1) * per_dev, LANES), jnp.bfloat16),
            pltpu.VMEM((2,) + weight.shape[1:], jnp.bfloat16),
        )
        + (pltpu.VMEM((total, width // 2 // CHUNKS), jnp.bfloat16),) * CHUNKS,
        in_specs=[ANY] * 4,
        out_specs=(VMEM,) * (3 + CHUNKS),
        scratch_shapes=[
            pltpu.VMEM(video.shape, jnp.bfloat16),
            pltpu.VMEM(text.shape, jnp.bfloat16),
            pltpu.VMEM(stale.shape, jnp.bfloat16),
            pltpu.VMEM((total, width), jnp.bfloat16),
            pltpu.SemaphoreType.DMA((4,)),
        ],
        compiler_params=PARAMS,
        name="prepare",
    )(*operands)


def project(normed_ref, wqk_ref, wv_ref, o_ref, kv_ref, rows, load=None):
    columns = wv_ref.shape[1]
    blocks = columns // LANES
    requests = normed_ref.shape[0] // rows
    for unit in range(requests * blocks, o_ref.shape[0]):
        o_ref[unit] = jnp.zeros(o_ref.shape[1:], o_ref.dtype)
    for part in range(3):
        if part == 2 and load is not None:
            load.wait()
        weight = wqk_ref[part] if part < 2 else wv_ref[...]
        acc = jnp.dot(normed_ref[...], weight, preferred_element_type=jnp.float32)
        if part:
            kv_ref[part - 1] = acc.astype(jnp.bfloat16)
        for request in range(requests):
            for block in range(blocks):
                o_ref[request * blocks + block, part * rows : (part + 1) * rows, :] = acc[
                    request * rows : (request + 1) * rows, block * LANES : (block + 1) * LANES
                ].astype(jnp.bfloat16)


def first_kernel(
    unit_ref,
    mod_0,
    mod_1,
    mod_2,
    mod_3,
    wqk_ref,
    w_ref,
    stale_ref,
    o_ref,
    kv_ref,
    mod_ref,
    wv_ref,
    pieces_ref,
    normed_ref,
    sem,
    *,
    rows,
):
    load = pltpu.make_async_copy(w_ref.at[2], wv_ref, sem)
    load.start()
    for index, piece in enumerate((mod_0, mod_1, mod_2, mod_3)):
        pieces_ref[lax.axis_index("mp") ^ index, 0:1, :] = piece[...]
    total, width = unit_ref.shape
    piece_width = mod_0.shape[1]
    for line in range(3):
        start = line * width
        while start < (line + 1) * width:
            slot, at = divmod(start, piece_width)
            count = min(piece_width - at, (line + 1) * width - start)
            to = start - line * width
            mod_ref[line : line + 1, to : to + count] = pieces_ref[slot, 0:1, at : at + count]
            start += count
    step = 16
    for start in range(0, total, step):
        normed = unit_ref[start : start + step, :] * (1.0 + mod_ref[1:2, :]) + mod_ref[0:1, :]
        normed_ref[start : start + step, :] = normed.astype(jnp.bfloat16)
    for unit in range(stale_ref.shape[0]):
        o_ref[unit, 3 * rows :, :] = stale_ref[unit]
    project(normed_ref, wqk_ref, wv_ref, o_ref, kv_ref, rows, load)


def first_call(unit, mods, weight_qk, weight, stale, rows, devices):
    total, width = unit.shape
    return pl.pallas_call(
        lambda *refs: first_kernel(*refs, rows=rows),
        out_shape=(
            jax.ShapeDtypeStruct((devices, 3 * rows + stale.shape[1], LANES), jnp.bfloat16),
            jax.ShapeDtypeStruct((2, total, weight.shape[2]), jnp.bfloat16),
            pltpu.VMEM((3, width), jnp.float32),
            pltpu.VMEM(weight.shape[1:], jnp.bfloat16),
        ),
        in_specs=[VMEM] * 6 + [ANY, VMEM],
        out_specs=(VMEM,) * 4,
        scratch_shapes=[
            pltpu.VMEM((4, 8, mods[0].shape[1]), jnp.float32),
            pltpu.VMEM((total, width), jnp.bfloat16),
            pltpu.SemaphoreType.DMA,
        ],
        compiler_params=PARAMS,
        name="first_qkv",
    )(unit, *mods, weight_qk, pltpu.with_memory_space_constraint(weight, pltpu.HBM), stale)


def second_kernel(
    mod_ref, wqk_ref, wv_ref, kv_0_ref, *refs, rows
):
    mine_refs, other_refs, before_refs = (refs[i * CHUNKS : (i + 1) * CHUNKS] for i in range(3))
    o_ref, kv_ref, *base_refs, x_ref, normed_ref = refs[3 * CHUNKS :]
    total, span = mine_refs[0].shape
    half = span * CHUNKS
    core = lax.axis_index("mp") % 2
    for chunk in range(CHUNKS):
        x_ref[:, pl.ds(pl.multiple_of(core * half + chunk * span, LANES), span)] = mine_refs[chunk][...]
        x_ref[:, pl.ds(pl.multiple_of((1 - core) * half + chunk * span, LANES), span)] = other_refs[chunk][...]
    step = 16
    for start in range(0, total, step):
        normed = centered(x_ref[start : start + step, :]) * (1.0 + mod_ref[1:2, :]) + mod_ref[0:1, :]
        normed_ref[start : start + step, :] = normed.astype(jnp.bfloat16)
    project(normed_ref, wqk_ref, wv_ref, o_ref, kv_ref, rows)
    is_first = lax.axis_index("section") == 0

    @pl.when(is_first)
    def _():
        kv_ref[...] = kv_0_ref[...]
        for base_ref, before_ref in zip(base_refs, before_refs):
            base_ref[...] = before_ref[...]

    @pl.when(jnp.logical_not(is_first))
    def _():
        for base_ref, mine_ref in zip(base_refs, mine_refs):
            base_ref[...] = mine_ref[...]


def second_call(mine, other, before, kv_0, mod, weight_qk, weight_v, rows, devices):
    total, span = mine[0].shape
    return pl.pallas_call(
        lambda *refs: second_kernel(*refs, rows=rows),
        out_shape=(
            jax.ShapeDtypeStruct((devices, 3 * rows, LANES), jnp.bfloat16),
            jax.ShapeDtypeStruct(kv_0.shape, jnp.bfloat16),
        )
        + (pltpu.VMEM((total, span), jnp.bfloat16),) * CHUNKS,
        in_specs=[VMEM] * (4 + 3 * CHUNKS),
        out_specs=(VMEM,) * (2 + CHUNKS),
        scratch_shapes=[pltpu.VMEM((total, 2 * CHUNKS * span), jnp.bfloat16)] * 2,
        compiler_params=PARAMS,
        name="second_qkv",
    )(mod, weight_qk, weight_v, kv_0, *mine, *other, *before)


def attention_kernel(*refs, rows, per_dev, patches, blocks):
    if len(refs) == 8:
        lens_ref, text_ref, recv_ref, stale_ref, w_ref, o_ref, w_vmem, sem = refs
        copy = pltpu.make_async_copy(w_ref, w_vmem, sem)
        copy.start()
    else:
        lens_ref, text_ref, recv_ref, stale_ref, o_ref = refs
        copy = None
    devices = recv_ref.shape[0]
    capacity = devices * per_dev

    def block(ref, base, index):
        start = base + index * per_dev
        return ref[:, start : start + per_dev, :].reshape(capacity, LANES)

    groups = patches + 1
    fresh_k = [block(recv_ref, rows, index) for index in range(groups)]
    fresh_v = [block(recv_ref, 2 * rows, index) for index in range(groups)]
    stale_base = 3 * rows
    stale_k = [None] + [block(stale_ref, stale_base, index) for index in range(patches - 1)]
    stale_base += (patches - 1) * per_dev
    stale_v = [None] + [block(stale_ref, stale_base, index) for index in range(patches - 1)]
    slot = lax.broadcasted_iota(jnp.int32, (1, groups * capacity), 1)
    limit = jnp.zeros((1, groups * capacity), jnp.int32)
    request = jnp.minimum(lax.axis_index("seq") // blocks, lens_ref.shape[0] - 1)
    for index in range(groups):
        length = lens_ref[request, index] if index < patches else text_ref[request]
        limit = jnp.where(slot >= index * capacity, length + index * capacity, limit)
    bias = jnp.where(slot < limit, 0.0, NEG)
    lane = lax.broadcasted_iota(jnp.int32, (1, LANES), 1)
    ones = jnp.ones((groups * capacity, LANES), jnp.bfloat16)
    factor = HEAD ** (-0.5) * math.log2(math.e)
    for patch in range(patches):
        keys = jnp.concatenate(
            [fresh_k[i] if i <= patch else stale_k[i] for i in range(patches)] + [fresh_k[patches]], axis=0
        )
        values = jnp.concatenate(
            [fresh_v[i] if i <= patch else stale_v[i] for i in range(patches)] + [fresh_v[patches]], axis=0
        )
        members = [patch, patches] if patch == 0 else [patch]
        queries = [block(recv_ref, 0, group) for group in members]
        queries = [jnp.where(lane < HEAD, q, jnp.zeros_like(q)) for q in queries] + [
            jnp.where(lane < HEAD, jnp.zeros_like(q), q) for q in queries
        ]
        scores = lax.dot_general(
            jnp.concatenate(queries, axis=0),
            keys,
            (((1,), (1,)), ((), ())),
            preferred_element_type=jnp.float32,
        )
        scores = scores * factor + bias
        top = jnp.max(scores, axis=-1, keepdims=True)
        weights = jnp.exp2(scores - top).astype(jnp.bfloat16)
        acc = jnp.dot(weights, jnp.concatenate([values, ones], axis=1), preferred_element_type=jnp.float32)
        acc = acc[:, :LANES] / acc[:, LANES:]
        for index, group in enumerate(members):
            lower = acc[index * capacity : (index + 1) * capacity]
            upper = acc[(len(members) + index) * capacity : (len(members) + index + 1) * capacity]
            out = jnp.where(lane < HEAD, lower, upper).astype(jnp.bfloat16)
            start = group * per_dev
            o_ref[:, start : start + per_dev, :] = out.reshape(devices, per_dev, LANES)
    if copy is not None:
        copy.wait()


def attention_call(lens, text_len, recv, stale, weight, rows, per_dev, blocks):
    devices = recv.shape[0]
    outs = jax.ShapeDtypeStruct((devices, rows, LANES), jnp.bfloat16)
    loads = weight is not None
    return pl.pallas_call(
        lambda *refs: attention_kernel(*refs, rows=rows, per_dev=per_dev, patches=lens.shape[1], blocks=blocks),
        out_shape=(outs, pltpu.VMEM(weight.shape, weight.dtype)) if loads else outs,
        in_specs=[SMEM, SMEM, VMEM, VMEM] + ([ANY] if loads else []),
        out_specs=(VMEM, VMEM) if loads else VMEM,
        scratch_shapes=[pltpu.SemaphoreType.DMA] if loads else [],
        compiler_params=PARAMS,
        name="attention",
    )(lens, text_len, recv, stale, *([pltpu.with_memory_space_constraint(weight, pltpu.HBM)] if loads else []))


def out_kernel(recv_ref, mod_ref, w_ref, *refs, last):
    *refs, mixed_ref = refs
    other_refs, mine_refs = refs[: len(refs) // 2], refs[len(refs) // 2 :]
    depth, width = w_ref.shape
    rows = recv_ref.shape[1]
    blocks = depth // LANES
    for request in range(mixed_ref.shape[0] // rows):
        for block in range(blocks):
            mixed_ref[request * rows : (request + 1) * rows, block * LANES : (block + 1) * LANES] = recv_ref[
                request * blocks + block
            ]
    half = width // 2
    span = half // len(other_refs)
    core = lax.axis_index("mp") % 2
    for refs, index in ((other_refs, 1 - core), (mine_refs, core)):
        for chunk, ref in enumerate(refs):
            at = pl.ds(pl.multiple_of(index * half + chunk * span, LANES), span)
            acc = jnp.dot(mixed_ref[...], w_ref[:, at], preferred_element_type=jnp.float32)
            acc = acc * mod_ref[2:3, at]
            if last:
                acc = jnp.where(lax.axis_index("section") == 0, jnp.zeros_like(acc), acc)
            ref[...] = acc.astype(ref.dtype)


def out_call(recv, mod, weight, requests, last):
    depth, width = weight.shape
    total = requests * recv.shape[1]
    return pl.pallas_call(
        lambda *refs: out_kernel(*refs, last=last),
        out_shape=[
            pltpu.VMEM((total, width // 2 // CHUNKS), dtype)
            for dtype in (jnp.bfloat16, jnp.float32)
            for _ in range(CHUNKS)
        ],
        in_specs=[VMEM, VMEM, VMEM],
        out_specs=[VMEM] * (2 * CHUNKS),
        scratch_shapes=[pltpu.VMEM((total, depth), jnp.bfloat16)],
        compiler_params=PARAMS,
        name="out_projection",
    )(recv, mod, weight)


def pick_kernel(arrived_ref, own_ref, o_ref):
    @pl.when(lax.axis_index("section") == 0)
    def _():
        o_ref[...] = own_ref[...]

    @pl.when(lax.axis_index("section") != 0)
    def _():
        o_ref[...] = arrived_ref[...]


def pick_call(arrived, own):
    return pl.pallas_call(
        pick_kernel,
        out_shape=pltpu.VMEM(own.shape, own.dtype),
        in_specs=[VMEM, VMEM],
        out_specs=VMEM,
        compiler_params=PARAMS,
        name="pick",
    )(arrived, own)


def cache_kernel(kv_ref, video_ref, text_ref):
    _, requests, patches, per_dev, _, _ = video_ref.shape
    row = 0
    for request in range(requests):
        for patch in range(patches + 1):
            for kind in range(2):
                values = kv_ref[kind, row : row + per_dev, :]
                if patch < patches:
                    video_ref[0, request, patch, :, kind, :] = values
                else:
                    text_ref[0, request, :, kind, :] = values
            row += per_dev


def cache_call(kv, video_shape, requests):
    per_dev, columns = video_shape[3], video_shape[5]
    return pl.pallas_call(
        cache_kernel,
        out_shape=(
            jax.ShapeDtypeStruct(video_shape, jnp.bfloat16),
            jax.ShapeDtypeStruct((1, requests, per_dev, 2, columns), jnp.bfloat16),
        ),
        in_specs=[VMEM],
        out_specs=(VMEM, VMEM),
        compiler_params=PARAMS,
        name="cache",
    )(kv)


def store_kernel(*refs):
    *pieces, video_ref, text_ref, sems = refs
    patches = video_ref.shape[2]
    span = pieces[0].shape[-1]
    half = span * CHUNKS
    core = lax.axis_index("mp") % 2
    copies = []
    for side, source in enumerate(pieces):
        index = core if side < CHUNKS else 1 - core
        at = pl.ds(pl.multiple_of(index * half + side % CHUNKS * span, LANES), span)
        copies.append(
            pltpu.make_async_copy(
                source.at[:, pl.ds(0, patches)], video_ref.at[0, :, :, :, at], sems.at[side, 0]
            )
        )
        copies.append(pltpu.make_async_copy(source.at[:, patches], text_ref.at[0, :, :, at], sems.at[side, 1]))
    for copy in copies:
        copy.start()
    for copy in copies:
        copy.wait()


def store_call(mine, other, video_shape, text_shape):
    _, requests, patches, per_dev, _ = video_shape
    pieces = [piece.reshape(requests, patches + 1, per_dev, -1) for piece in mine + other]
    return pl.pallas_call(
        store_kernel,
        out_shape=(
            jax.ShapeDtypeStruct(video_shape, jnp.bfloat16),
            jax.ShapeDtypeStruct(text_shape, jnp.bfloat16),
        ),
        in_specs=[VMEM] * (2 * CHUNKS),
        out_specs=(ANY, ANY),
        scratch_shapes=[pltpu.SemaphoreType.DMA((2 * CHUNKS, 2))],
        compiler_params=PARAMS,
        name="store",
    )(*pieces)


def body(video, text, patch_lengths, text_len, timestep, w_mod, w_qkv, w_out, stale_cache):
    devices = lax.axis_size("seq")
    requests, patches, per_dev, _ = video.shape
    blocks = w_out.shape[1] // LANES
    rows = patches * per_dev + text.shape[1]

    own_mod = modulation(timestep, w_mod[0])
    mods = [own_mod] + [
        swap(own_mod, lambda section, part, flip=flip: (section, part ^ flip)) for flip in (1, 2, 3)
    ]
    weight = w_qkv[0].transpose(1, 0, 2)
    unit, stale, weight_qk, *x_half = prepare_call(video, text, weight, stale_cache[0])

    def reduced(mixed, weight_out, mod, last):
        pieces = out_call(mixed, mod, weight_out, requests, last)
        return [
            (mine + swap_core(other).astype(jnp.float32)).astype(jnp.bfloat16)
            for other, mine in zip(pieces[:CHUNKS], pieces[CHUNKS:])
        ]

    def added(x_half, on_chip, arrived):
        return [
            (a.astype(jnp.float32) + (b.astype(jnp.float32) + c.astype(jnp.float32))).astype(jnp.bfloat16)
            for a, b, c in zip(x_half, on_chip, arrived)
        ]

    def each(function, values):
        return [function(value) for value in values]

    sent_0, kv_0, mod, weight_v = first_call(unit, mods, weight_qk, weight, stale, rows, devices)
    recv_0 = lax.all_to_all(sent_0, "seq", 0, 0, tiled=True)
    weight_out = w_out[0]
    attended = attention_call(patch_lengths, text_len, recv_0, recv_0, None, rows, per_dev, blocks)
    on_chip = reduced(lax.all_to_all(attended, "seq", 0, 0, tiled=True), weight_out, mod, False)
    crossed = pick_call(next_section(on_chip[1]), on_chip[1])
    result_0 = added(x_half, [on_chip[0], crossed], [swap_chip(on_chip[0]), swap_chip(crossed)])

    x_half = [next_section(result_0[0]), result_0[1]]
    sent_1, key_value, *base = second_call(
        x_half, each(swap_core, x_half), result_0, kv_0, mod, weight_qk, weight_v, rows, devices
    )
    recv_1 = lax.all_to_all(sent_1, "seq", 0, 0, tiled=True)
    attended = attention_call(patch_lengths, text_len, recv_1, recv_0, None, rows, per_dev, blocks)
    on_chip = reduced(lax.all_to_all(attended, "seq", 0, 0, tiled=True), weight_out, mod, True)
    arrived = each(swap_chip, on_chip)
    arrived[0], key_value = lax.optimization_barrier((arrived[0], key_value))

    cache_video, cache_text = cache_call(key_value, (1,) + stale_cache.shape[1:], requests)
    result = added(base, on_chip, arrived)
    hidden_video, hidden_text = store_call(result, each(swap_core, result), (1,) + video.shape, (1,) + text.shape)
    return (hidden_video, hidden_text, cache_video, cache_text)


def solution(mesh):
    placed = (
        P(None, None, "seq", None),
        P(None, "seq", None),
        P(),
        P(),
        P(),
        P("section", None, "mp"),
        P("section", None, None, "mp"),
        P("section", "mp", None),
        P("section", None, None, "seq", None, "mp"),
    )
    return jax.shard_map(
        body,
        mesh=mesh,
        in_specs=placed,
        out_specs=(
            P("section", None, None, "seq", None),
            P("section", None, "seq", None),
            P("section", None, None, "seq", None, "mp"),
            P("section", None, "seq", None, "mp"),
        ),
        check_vma=False,
    )
```

```python
import math

import jax
import jax.numpy as jnp
from jax import lax
from jax.experimental import pallas as pl
from jax.experimental.pallas import tpu as pltpu
from jax.sharding import PartitionSpec as P

HEAD = 64
LANES = 128
EPS = 1e-05
NEG = -1e30
CHUNKS = 2
VMEM_LIMIT = 12 * 1024 * 1024


def modulation(timestep, weight):
    half_width = weight.shape[0] // 2
    frequency = jnp.exp(-math.log(10000.0) * jnp.arange(half_width, dtype=jnp.float32) / half_width)
    phases = timestep.astype(jnp.float32)[0] * frequency
    embedding = jnp.concatenate([jnp.cos(phases), jnp.sin(phases)])
    active = jax.nn.silu(embedding).astype(jnp.bfloat16)
    return jnp.dot(active[None, :], weight, preferred_element_type=jnp.float32)


def swap(value, mapping):
    pairs = []
    for section in range(2):
        for part in range(4):
            target = mapping(section, part)
            pairs.append((section * 4 + part, target[0] * 4 + target[1]))
    return lax.ppermute(value, ("section", "mp"), pairs)


def swap_core(value):
    return swap(value, lambda section, part: (section, part ^ 1))


def swap_chip(value):
    return swap(value, lambda section, part: (section, part ^ 2))


def next_section(value):
    return swap(value, lambda section, part: (1 - section, part ^ 2))

VMEM = pl.BlockSpec(memory_space=pltpu.VMEM)
SMEM = pl.BlockSpec(memory_space=pltpu.SMEM)
ANY = pl.BlockSpec(memory_space=pl.ANY)
PARAMS = pltpu.CompilerParams(vmem_limit_bytes=VMEM_LIMIT)


def centered(values):
    values = values.astype(jnp.float32)
    center = values - jnp.mean(values, axis=-1, keepdims=True)
    spread = jnp.mean(center * center, axis=-1, keepdims=True)
    return center * lax.rsqrt(spread + EPS)


def prepare_kernel(
    video_ref, text_ref, w_ref, stale_ref, unit_ref, packed_ref, w_vmem, *refs
):
    *half_refs, video_buf, text_buf, stale_buf, x_ref, sems = refs
    requests, patches, per_dev, width = video_ref.shape
    first = [
        pltpu.make_async_copy(stale_ref, stale_buf, sems.at[0]),
        pltpu.make_async_copy(video_ref, video_buf, sems.at[1]),
        pltpu.make_async_copy(text_ref, text_buf, sems.at[2]),
    ]
    load = pltpu.make_async_copy(w_ref.at[pl.ds(0, 2)], w_vmem, sems.at[3])
    for copy in first + [load]:
        copy.start()
    first[0].wait()
    blocks = w_ref.shape[2] // LANES
    for request in range(requests):
        for patch in range(1, patches):
            both = stale_buf[request, patch]
            for kind in range(2):
                values = both[:, kind, :]
                row = (kind * (patches - 1) + patch - 1) * per_dev
                for block in range(blocks):
                    packed_ref[request * blocks + block, row : row + per_dev, :] = values[
                        :, block * LANES : (block + 1) * LANES
                    ]
    for copy in first[1:]:
        copy.wait()
    row = 0
    for request in range(requests):
        for patch in range(patches + 1):
            values = video_buf[request, patch] if patch < patches else text_buf[request]
            x_ref[row : row + per_dev, :] = values
            unit_ref[row : row + per_dev, :] = centered(values)
            row += per_dev
    half = width // 2
    core = lax.axis_index("mp") % 2
    span = half // len(half_refs)
    for chunk, ref in enumerate(half_refs):
        ref[...] = x_ref[:, pl.ds(pl.multiple_of(core * half + chunk * span, LANES), span)]
    load.wait()


def prepare_call(video, text, weight, stale):
    requests, patches, per_dev, width = video.shape
    total = requests * (patches + 1) * per_dev
    units = requests * (weight.shape[2] // LANES)
    operands = [pltpu.with_memory_space_constraint(value, pltpu.HBM) for value in (video, text, weight, stale)]
    return pl.pallas_call(
        prepare_kernel,
        out_shape=(
            pltpu.VMEM((total, width), jnp.float32),
            pltpu.VMEM((units, 2 * (patches - 1) * per_dev, LANES), jnp.bfloat16),
            pltpu.VMEM((2,) + weight.shape[1:], jnp.bfloat16),
        )
        + (pltpu.VMEM((total, width // 2 // CHUNKS), jnp.bfloat16),) * CHUNKS,
        in_specs=[ANY] * 4,
        out_specs=(VMEM,) * (3 + CHUNKS),
        scratch_shapes=[
            pltpu.VMEM(video.shape, jnp.bfloat16),
            pltpu.VMEM(text.shape, jnp.bfloat16),
            pltpu.VMEM(stale.shape, jnp.bfloat16),
            pltpu.VMEM((total, width), jnp.bfloat16),
            pltpu.SemaphoreType.DMA((4,)),
        ],
        compiler_params=PARAMS,
        name="prepare",
    )(*operands)


def project(normed_ref, wqk_ref, wv_ref, o_ref, kv_ref, rows, load=None):
    columns = wv_ref.shape[1]
    blocks = columns // LANES
    requests = normed_ref.shape[0] // rows
    for unit in range(requests * blocks, o_ref.shape[0]):
        o_ref[unit] = jnp.zeros(o_ref.shape[1:], o_ref.dtype)
    for part in range(3):
        if part == 2 and load is not None:
            load.wait()
        weight = wqk_ref[part] if part < 2 else wv_ref[...]
        acc = jnp.dot(normed_ref[...], weight, preferred_element_type=jnp.float32)
        if part:
            kv_ref[part - 1] = acc.astype(jnp.bfloat16)
        for request in range(requests):
            for block in range(blocks):
                o_ref[request * blocks + block, part * rows : (part + 1) * rows, :] = acc[
                    request * rows : (request + 1) * rows, block * LANES : (block + 1) * LANES
                ].astype(jnp.bfloat16)


def first_kernel(
    unit_ref,
    mod_0,
    mod_1,
    mod_2,
    mod_3,
    wqk_ref,
    w_ref,
    stale_ref,
    o_ref,
    kv_ref,
    mod_ref,
    wv_ref,
    pieces_ref,
    normed_ref,
    sem,
    *,
    rows,
):
    load = pltpu.make_async_copy(w_ref.at[2], wv_ref, sem)
    load.start()
    for index, piece in enumerate((mod_0, mod_1, mod_2, mod_3)):
        pieces_ref[lax.axis_index("mp") ^ index, 0:1, :] = piece[...]
    total, width = unit_ref.shape
    piece_width = mod_0.shape[1]
    for line in range(3):
        start = line * width
        while start < (line + 1) * width:
            slot, at = divmod(start, piece_width)
            count = min(piece_width - at, (line + 1) * width - start)
            to = start - line * width
            mod_ref[line : line + 1, to : to + count] = pieces_ref[slot, 0:1, at : at + count]
            start += count
    step = 16
    for start in range(0, total, step):
        normed = unit_ref[start : start + step, :] * (1.0 + mod_ref[1:2, :]) + mod_ref[0:1, :]
        normed_ref[start : start + step, :] = normed.astype(jnp.bfloat16)
    for unit in range(stale_ref.shape[0]):
        o_ref[unit, 3 * rows :, :] = stale_ref[unit]
    project(normed_ref, wqk_ref, wv_ref, o_ref, kv_ref, rows, load)


def first_call(unit, mods, weight_qk, weight, stale, rows, devices):
    total, width = unit.shape
    return pl.pallas_call(
        lambda *refs: first_kernel(*refs, rows=rows),
        out_shape=(
            jax.ShapeDtypeStruct((devices, 3 * rows + stale.shape[1], LANES), jnp.bfloat16),
            jax.ShapeDtypeStruct((2, total, weight.shape[2]), jnp.bfloat16),
            pltpu.VMEM((3, width), jnp.float32),
            pltpu.VMEM(weight.shape[1:], jnp.bfloat16),
        ),
        in_specs=[VMEM] * 6 + [ANY, VMEM],
        out_specs=(VMEM,) * 4,
        scratch_shapes=[
            pltpu.VMEM((4, 8, mods[0].shape[1]), jnp.float32),
            pltpu.VMEM((total, width), jnp.bfloat16),
            pltpu.SemaphoreType.DMA,
        ],
        compiler_params=PARAMS,
        name="first_qkv",
    )(unit, *mods, weight_qk, pltpu.with_memory_space_constraint(weight, pltpu.HBM), stale)


def second_kernel(
    mod_ref, wqk_ref, wv_ref, kv_0_ref, *refs, rows
):
    mine_refs, other_refs, before_refs = (refs[i * CHUNKS : (i + 1) * CHUNKS] for i in range(3))
    o_ref, kv_ref, *base_refs, x_ref, normed_ref = refs[3 * CHUNKS :]
    total, span = mine_refs[0].shape
    half = span * CHUNKS
    core = lax.axis_index("mp") % 2
    for chunk in range(CHUNKS):
        x_ref[:, pl.ds(pl.multiple_of(core * half + chunk * span, LANES), span)] = mine_refs[chunk][...]
        x_ref[:, pl.ds(pl.multiple_of((1 - core) * half + chunk * span, LANES), span)] = other_refs[chunk][...]
    step = 16
    for start in range(0, total, step):
        normed = centered(x_ref[start : start + step, :]) * (1.0 + mod_ref[1:2, :]) + mod_ref[0:1, :]
        normed_ref[start : start + step, :] = normed.astype(jnp.bfloat16)
    project(normed_ref, wqk_ref, wv_ref, o_ref, kv_ref, rows)
    is_first = lax.axis_index("section") == 0

    @pl.when(is_first)
    def _():
        kv_ref[...] = kv_0_ref[...]
        for base_ref, before_ref in zip(base_refs, before_refs):
            base_ref[...] = before_ref[...]

    @pl.when(jnp.logical_not(is_first))
    def _():
        for base_ref, mine_ref in zip(base_refs, mine_refs):
            base_ref[...] = mine_ref[...]


def second_call(mine, other, before, kv_0, mod, weight_qk, weight_v, rows, devices):
    total, span = mine[0].shape
    return pl.pallas_call(
        lambda *refs: second_kernel(*refs, rows=rows),
        out_shape=(
            jax.ShapeDtypeStruct((devices, 3 * rows, LANES), jnp.bfloat16),
            jax.ShapeDtypeStruct(kv_0.shape, jnp.bfloat16),
        )
        + (pltpu.VMEM((total, span), jnp.bfloat16),) * CHUNKS,
        in_specs=[VMEM] * (4 + 3 * CHUNKS),
        out_specs=(VMEM,) * (2 + CHUNKS),
        scratch_shapes=[pltpu.VMEM((total, 2 * CHUNKS * span), jnp.bfloat16)] * 2,
        compiler_params=PARAMS,
        name="second_qkv",
    )(mod, weight_qk, weight_v, kv_0, *mine, *other, *before)


def attention_kernel(*refs, rows, per_dev, patches, blocks):
    if len(refs) == 8:
        lens_ref, text_ref, recv_ref, stale_ref, w_ref, o_ref, w_vmem, sem = refs
        copy = pltpu.make_async_copy(w_ref, w_vmem, sem)
        copy.start()
    else:
        lens_ref, text_ref, recv_ref, stale_ref, o_ref = refs
        copy = None
    devices = recv_ref.shape[0]
    capacity = devices * per_dev

    def block(ref, base, index):
        start = base + index * per_dev
        return ref[:, start : start + per_dev, :].reshape(capacity, LANES)

    groups = patches + 1
    fresh_k = [block(recv_ref, rows, index) for index in range(groups)]
    fresh_v = [block(recv_ref, 2 * rows, index) for index in range(groups)]
    stale_base = 3 * rows
    stale_k = [None] + [block(stale_ref, stale_base, index) for index in range(patches - 1)]
    stale_base += (patches - 1) * per_dev
    stale_v = [None] + [block(stale_ref, stale_base, index) for index in range(patches - 1)]
    slot = lax.broadcasted_iota(jnp.int32, (1, groups * capacity), 1)
    limit = jnp.zeros((1, groups * capacity), jnp.int32)
    request = jnp.minimum(lax.axis_index("seq") // blocks, lens_ref.shape[0] - 1)
    for index in range(groups):
        length = lens_ref[request, index] if index < patches else text_ref[request]
        limit = jnp.where(slot >= index * capacity, length + index * capacity, limit)
    bias = jnp.where(slot < limit, 0.0, NEG)
    lane = lax.broadcasted_iota(jnp.int32, (1, LANES), 1)
    ones = jnp.ones((groups * capacity, LANES), jnp.bfloat16)
    factor = HEAD ** (-0.5) * math.log2(math.e)
    for patch in range(patches):
        keys = jnp.concatenate(
            [fresh_k[i] if i <= patch else stale_k[i] for i in range(patches)] + [fresh_k[patches]], axis=0
        )
        values = jnp.concatenate(
            [fresh_v[i] if i <= patch else stale_v[i] for i in range(patches)] + [fresh_v[patches]], axis=0
        )
        members = [patch, patches] if patch == 0 else [patch]
        queries = [block(recv_ref, 0, group) for group in members]
        queries = [jnp.where(lane < HEAD, q, jnp.zeros_like(q)) for q in queries] + [
            jnp.where(lane < HEAD, jnp.zeros_like(q), q) for q in queries
        ]
        scores = lax.dot_general(
            jnp.concatenate(queries, axis=0),
            keys,
            (((1,), (1,)), ((), ())),
            preferred_element_type=jnp.float32,
        )
        scores = scores * factor + bias
        top = jnp.max(scores, axis=-1, keepdims=True)
        weights = jnp.exp2(scores - top).astype(jnp.bfloat16)
        acc = jnp.dot(weights, jnp.concatenate([values, ones], axis=1), preferred_element_type=jnp.float32)
        acc = acc[:, :LANES] / acc[:, LANES:]
        for index, group in enumerate(members):
            lower = acc[index * capacity : (index + 1) * capacity]
            upper = acc[(len(members) + index) * capacity : (len(members) + index + 1) * capacity]
            out = jnp.where(lane < HEAD, lower, upper).astype(jnp.bfloat16)
            start = group * per_dev
            o_ref[:, start : start + per_dev, :] = out.reshape(devices, per_dev, LANES)
    if copy is not None:
        copy.wait()


def attention_call(lens, text_len, recv, stale, weight, rows, per_dev, blocks):
    devices = recv.shape[0]
    outs = jax.ShapeDtypeStruct((devices, rows, LANES), jnp.bfloat16)
    loads = weight is not None
    return pl.pallas_call(
        lambda *refs: attention_kernel(*refs, rows=rows, per_dev=per_dev, patches=lens.shape[1], blocks=blocks),
        out_shape=(outs, pltpu.VMEM(weight.shape, weight.dtype)) if loads else outs,
        in_specs=[SMEM, SMEM, VMEM, VMEM] + ([ANY] if loads else []),
        out_specs=(VMEM, VMEM) if loads else VMEM,
        scratch_shapes=[pltpu.SemaphoreType.DMA] if loads else [],
        compiler_params=PARAMS,
        name="attention",
    )(lens, text_len, recv, stale, *([pltpu.with_memory_space_constraint(weight, pltpu.HBM)] if loads else []))


def out_kernel(recv_ref, mod_ref, w_ref, *refs, mine, last):
    *refs, mixed_ref = refs
    depth, width = w_ref.shape
    rows = recv_ref.shape[1]
    blocks = depth // LANES
    for request in range(mixed_ref.shape[0] // rows):
        for block in range(blocks):
            mixed_ref[request * rows : (request + 1) * rows, block * LANES : (block + 1) * LANES] = recv_ref[
                request * blocks + block
            ]
    half = width // 2
    span = half // len(refs)
    core = lax.axis_index("mp") % 2
    index = core if mine else 1 - core
    for chunk, ref in enumerate(refs):
        at = pl.ds(pl.multiple_of(index * half + chunk * span, LANES), span)
        acc = jnp.dot(mixed_ref[...], w_ref[:, at], preferred_element_type=jnp.float32)
        acc = acc * mod_ref[2:3, at]
        if last:
            acc = jnp.where(lax.axis_index("section") == 0, jnp.zeros_like(acc), acc)
        ref[...] = acc.astype(ref.dtype)


def out_call(recv, mod, weight, requests, mine, last):
    depth, width = weight.shape
    total = requests * recv.shape[1]
    return pl.pallas_call(
        lambda *refs: out_kernel(*refs, mine=mine, last=last),
        out_shape=[
            pltpu.VMEM((total, width // 2 // CHUNKS), jnp.float32 if mine else jnp.bfloat16)
            for _ in range(CHUNKS)
        ],
        in_specs=[VMEM, VMEM, VMEM],
        out_specs=[VMEM] * CHUNKS,
        scratch_shapes=[pltpu.VMEM((total, depth), jnp.bfloat16)],
        compiler_params=PARAMS,
        name="out_projection",
    )(recv, mod, weight)


def pick_kernel(arrived_ref, own_ref, o_ref):
    @pl.when(lax.axis_index("section") == 0)
    def _():
        o_ref[...] = own_ref[...]

    @pl.when(lax.axis_index("section") != 0)
    def _():
        o_ref[...] = arrived_ref[...]


def pick_call(arrived, own):
    return pl.pallas_call(
        pick_kernel,
        out_shape=pltpu.VMEM(own.shape, own.dtype),
        in_specs=[VMEM, VMEM],
        out_specs=VMEM,
        compiler_params=PARAMS,
        name="pick",
    )(arrived, own)


def cache_kernel(kv_ref, video_ref, text_ref):
    _, requests, patches, per_dev, _, _ = video_ref.shape
    row = 0
    for request in range(requests):
        for patch in range(patches + 1):
            for kind in range(2):
                values = kv_ref[kind, row : row + per_dev, :]
                if patch < patches:
                    video_ref[0, request, patch, :, kind, :] = values
                else:
                    text_ref[0, request, :, kind, :] = values
            row += per_dev


def cache_call(kv, video_shape, requests):
    per_dev, columns = video_shape[3], video_shape[5]
    return pl.pallas_call(
        cache_kernel,
        out_shape=(
            jax.ShapeDtypeStruct(video_shape, jnp.bfloat16),
            jax.ShapeDtypeStruct((1, requests, per_dev, 2, columns), jnp.bfloat16),
        ),
        in_specs=[VMEM],
        out_specs=(VMEM, VMEM),
        compiler_params=PARAMS,
        name="cache",
    )(kv)


def store_kernel(*refs):
    *pieces, video_ref, text_ref, sems = refs
    patches = video_ref.shape[2]
    span = pieces[0].shape[-1]
    half = span * CHUNKS
    core = lax.axis_index("mp") % 2
    copies = []
    for side, source in enumerate(pieces):
        index = core if side < CHUNKS else 1 - core
        at = pl.ds(pl.multiple_of(index * half + side % CHUNKS * span, LANES), span)
        copies.append(
            pltpu.make_async_copy(
                source.at[:, pl.ds(0, patches)], video_ref.at[0, :, :, :, at], sems.at[side, 0]
            )
        )
        copies.append(pltpu.make_async_copy(source.at[:, patches], text_ref.at[0, :, :, at], sems.at[side, 1]))
    for copy in copies:
        copy.start()
    for copy in copies:
        copy.wait()


def store_call(mine, other, video_shape, text_shape):
    _, requests, patches, per_dev, _ = video_shape
    pieces = [piece.reshape(requests, patches + 1, per_dev, -1) for piece in mine + other]
    return pl.pallas_call(
        store_kernel,
        out_shape=(
            jax.ShapeDtypeStruct(video_shape, jnp.bfloat16),
            jax.ShapeDtypeStruct(text_shape, jnp.bfloat16),
        ),
        in_specs=[VMEM] * (2 * CHUNKS),
        out_specs=(ANY, ANY),
        scratch_shapes=[pltpu.SemaphoreType.DMA((2 * CHUNKS, 2))],
        compiler_params=PARAMS,
        name="store",
    )(*pieces)


def body(video, text, patch_lengths, text_len, timestep, w_mod, w_qkv, w_out, stale_cache):
    devices = lax.axis_size("seq")
    requests, patches, per_dev, _ = video.shape
    blocks = w_out.shape[1] // LANES
    rows = patches * per_dev + text.shape[1]

    own_mod = modulation(timestep, w_mod[0])
    mods = [own_mod] + [
        swap(own_mod, lambda section, part, flip=flip: (section, part ^ flip)) for flip in (1, 2, 3)
    ]
    weight = w_qkv[0].transpose(1, 0, 2)
    unit, stale, weight_qk, *x_half = prepare_call(video, text, weight, stale_cache[0])

    def reduced(mixed, weight_out, mod, last):
        others = each(swap_core, out_call(mixed, mod, weight_out, requests, False, last))
        mines = out_call(mixed, mod, weight_out, requests, True, last)
        return [(a + b.astype(jnp.float32)).astype(jnp.bfloat16) for a, b in zip(mines, others)]

    def added(x_half, on_chip, arrived):
        return [
            (a.astype(jnp.float32) + (b.astype(jnp.float32) + c.astype(jnp.float32))).astype(jnp.bfloat16)
            for a, b, c in zip(x_half, on_chip, arrived)
        ]

    def each(function, values):
        return [function(value) for value in values]

    sent_0, kv_0, mod, weight_v = first_call(unit, mods, weight_qk, weight, stale, rows, devices)
    recv_0 = lax.all_to_all(sent_0, "seq", 0, 0, tiled=True)
    weight_out = w_out[0]
    attended = attention_call(patch_lengths, text_len, recv_0, recv_0, None, rows, per_dev, blocks)
    on_chip = reduced(lax.all_to_all(attended, "seq", 0, 0, tiled=True), weight_out, mod, False)
    crossed = pick_call(next_section(on_chip[0]), on_chip[0])
    result_0 = added(x_half, [crossed, on_chip[1]], [swap_chip(crossed), swap_chip(on_chip[1])])

    x_half = [result_0[0], next_section(result_0[1])]
    sent_1, key_value, *base = second_call(
        x_half, each(swap_core, x_half), result_0, kv_0, mod, weight_qk, weight_v, rows, devices
    )
    recv_1 = lax.all_to_all(sent_1, "seq", 0, 0, tiled=True)
    attended = attention_call(patch_lengths, text_len, recv_1, recv_0, None, rows, per_dev, blocks)
    on_chip = reduced(lax.all_to_all(attended, "seq", 0, 0, tiled=True), weight_out, mod, True)
    arrived = each(swap_chip, on_chip)
    arrived[0], key_value = lax.optimization_barrier((arrived[0], key_value))

    cache_video, cache_text = cache_call(key_value, (1,) + stale_cache.shape[1:], requests)
    result = added(base, on_chip, arrived)
    hidden_video, hidden_text = store_call(result, each(swap_core, result), (1,) + video.shape, (1,) + text.shape)
    return (hidden_video, hidden_text, cache_video, cache_text)


def solution(mesh):
    placed = (
        P(None, None, "seq", None),
        P(None, "seq", None),
        P(),
        P(),
        P(),
        P("section", None, "mp"),
        P("section", None, None, "mp"),
        P("section", "mp", None),
        P("section", None, None, "seq", None, "mp"),
    )
    return jax.shard_map(
        body,
        mesh=mesh,
        in_specs=placed,
        out_specs=(
            P("section", None, None, "seq", None),
            P("section", None, "seq", None),
            P("section", None, None, "seq", None, "mp"),
            P("section", None, "seq", None, "mp"),
        ),
        check_vma=False,
    )
```

```python
import math

import jax
import jax.numpy as jnp
from jax import lax
from jax.experimental import pallas as pl
from jax.experimental.pallas import tpu as pltpu
from jax.sharding import PartitionSpec as P

HEAD = 64
LANES = 128
EPS = 1e-05
NEG = -1e30
CHUNKS = 2
WIDE = 256
VMEM_LIMIT = 12 * 1024 * 1024


def modulation(timestep, weight):
    half_width = weight.shape[0] // 2
    frequency = jnp.exp(-math.log(10000.0) * jnp.arange(half_width, dtype=jnp.float32) / half_width)
    phases = timestep.astype(jnp.float32)[0] * frequency
    embedding = jnp.concatenate([jnp.cos(phases), jnp.sin(phases)])
    active = jax.nn.silu(embedding).astype(jnp.bfloat16)
    return jnp.dot(active[None, :], weight, preferred_element_type=jnp.float32)


def swap(value, mapping):
    pairs = []
    for section in range(2):
        for part in range(4):
            target = mapping(section, part)
            pairs.append((section * 4 + part, target[0] * 4 + target[1]))
    return lax.ppermute(value, ("section", "mp"), pairs)


def swap_core(value):
    return swap(value, lambda section, part: (section, part ^ 1))


def swap_chip(value):
    return swap(value, lambda section, part: (section, part ^ 2))


def next_section(value):
    return swap(value, lambda section, part: (1 - section, part ^ 2))

VMEM = pl.BlockSpec(memory_space=pltpu.VMEM)
SMEM = pl.BlockSpec(memory_space=pltpu.SMEM)
ANY = pl.BlockSpec(memory_space=pl.ANY)
PARAMS = pltpu.CompilerParams(vmem_limit_bytes=VMEM_LIMIT)


def centered(values):
    values = values.astype(jnp.float32)
    center = values - jnp.mean(values, axis=-1, keepdims=True)
    spread = jnp.mean(center * center, axis=-1, keepdims=True)
    return center * lax.rsqrt(spread + EPS)


def prepare_kernel(
    video_ref, text_ref, w_ref, stale_ref, unit_ref, packed_ref, w_vmem, *refs
):
    *half_refs, video_buf, text_buf, stale_buf, x_ref, sems = refs
    requests, patches, per_dev, width = video_ref.shape
    first = [
        pltpu.make_async_copy(stale_ref, stale_buf, sems.at[0]),
        pltpu.make_async_copy(video_ref, video_buf, sems.at[1]),
        pltpu.make_async_copy(text_ref, text_buf, sems.at[2]),
    ]
    load = pltpu.make_async_copy(w_ref.at[pl.ds(0, 2)], w_vmem, sems.at[3])
    for copy in first + [load]:
        copy.start()
    first[0].wait()
    blocks = w_ref.shape[2] // LANES
    for request in range(requests):
        for patch in range(1, patches):
            both = stale_buf[request, patch]
            for kind in range(2):
                values = both[:, kind, :]
                row = (kind * (patches - 1) + patch - 1) * per_dev
                for block in range(blocks):
                    packed_ref[request * blocks + block, row : row + per_dev, :] = values[
                        :, block * LANES : (block + 1) * LANES
                    ]
    for copy in first[1:]:
        copy.wait()
    row = 0
    for request in range(requests):
        for patch in range(patches + 1):
            values = video_buf[request, patch] if patch < patches else text_buf[request]
            x_ref[row : row + per_dev, :] = values
            unit_ref[row : row + per_dev, :] = centered(values)
            row += per_dev
    half = width // 2
    core = lax.axis_index("mp") % 2
    span = half // len(half_refs)
    for chunk, ref in enumerate(half_refs):
        ref[...] = x_ref[:, pl.ds(pl.multiple_of(core * half + chunk * span, LANES), span)]
    load.wait()


def prepare_call(video, text, weight, stale):
    requests, patches, per_dev, width = video.shape
    total = requests * (patches + 1) * per_dev
    units = requests * (weight.shape[2] // LANES)
    operands = [pltpu.with_memory_space_constraint(value, pltpu.HBM) for value in (video, text, weight, stale)]
    return pl.pallas_call(
        prepare_kernel,
        out_shape=(
            pltpu.VMEM((total, width), jnp.float32),
            pltpu.VMEM((units, 2 * (patches - 1) * per_dev, LANES), jnp.bfloat16),
            pltpu.VMEM((2,) + weight.shape[1:], jnp.bfloat16),
        )
        + (pltpu.VMEM((total, width // 2 // CHUNKS), jnp.bfloat16),) * CHUNKS,
        in_specs=[ANY] * 4,
        out_specs=(VMEM,) * (3 + CHUNKS),
        scratch_shapes=[
            pltpu.VMEM(video.shape, jnp.bfloat16),
            pltpu.VMEM(text.shape, jnp.bfloat16),
            pltpu.VMEM(stale.shape, jnp.bfloat16),
            pltpu.VMEM((total, width), jnp.bfloat16),
            pltpu.SemaphoreType.DMA((4,)),
        ],
        compiler_params=PARAMS,
        name="prepare",
    )(*operands)


def project(normed_ref, wqk_ref, wv_ref, o_ref, kv_ref, rows, load=None):
    columns = wv_ref.shape[1]
    blocks = columns // LANES
    requests = normed_ref.shape[0] // rows
    for unit in range(requests * blocks, o_ref.shape[0]):
        o_ref[unit] = jnp.zeros(o_ref.shape[1:], o_ref.dtype)
    for part in range(3):
        if part == 2 and load is not None:
            load.wait()
        for wide in range(0, columns, WIDE):
            at = slice(wide, wide + WIDE)
            weight = wqk_ref[part, :, at] if part < 2 else wv_ref[:, at]
            acc = jnp.dot(normed_ref[...], weight, preferred_element_type=jnp.float32).astype(jnp.bfloat16)
            if part:
                kv_ref[part - 1, :, at] = acc
            for request in range(requests):
                for block in range(WIDE // LANES):
                    unit = request * blocks + wide // LANES + block
                    o_ref[unit, part * rows : (part + 1) * rows, :] = acc[
                        request * rows : (request + 1) * rows, block * LANES : (block + 1) * LANES
                    ]


def first_kernel(
    unit_ref,
    mod_0,
    mod_1,
    mod_2,
    mod_3,
    wqk_ref,
    w_ref,
    stale_ref,
    o_ref,
    kv_ref,
    mod_ref,
    wv_ref,
    pieces_ref,
    normed_ref,
    sem,
    *,
    rows,
):
    load = pltpu.make_async_copy(w_ref.at[2], wv_ref, sem)
    load.start()
    for index, piece in enumerate((mod_0, mod_1, mod_2, mod_3)):
        pieces_ref[lax.axis_index("mp") ^ index, 0:1, :] = piece[...]
    total, width = unit_ref.shape
    piece_width = mod_0.shape[1]
    for line in range(3):
        start = line * width
        while start < (line + 1) * width:
            slot, at = divmod(start, piece_width)
            count = min(piece_width - at, (line + 1) * width - start)
            to = start - line * width
            mod_ref[line : line + 1, to : to + count] = pieces_ref[slot, 0:1, at : at + count]
            start += count
    step = 16
    for start in range(0, total, step):
        normed = unit_ref[start : start + step, :] * (1.0 + mod_ref[1:2, :]) + mod_ref[0:1, :]
        normed_ref[start : start + step, :] = normed.astype(jnp.bfloat16)
    for unit in range(stale_ref.shape[0]):
        o_ref[unit, 3 * rows :, :] = stale_ref[unit]
    project(normed_ref, wqk_ref, wv_ref, o_ref, kv_ref, rows, load)


def first_call(unit, mods, weight_qk, weight, stale, rows, devices):
    total, width = unit.shape
    return pl.pallas_call(
        lambda *refs: first_kernel(*refs, rows=rows),
        out_shape=(
            jax.ShapeDtypeStruct((devices, 3 * rows + stale.shape[1], LANES), jnp.bfloat16),
            jax.ShapeDtypeStruct((2, total, weight.shape[2]), jnp.bfloat16),
            pltpu.VMEM((3, width), jnp.float32),
            pltpu.VMEM(weight.shape[1:], jnp.bfloat16),
        ),
        in_specs=[VMEM] * 6 + [ANY, VMEM],
        out_specs=(VMEM,) * 4,
        scratch_shapes=[
            pltpu.VMEM((4, 8, mods[0].shape[1]), jnp.float32),
            pltpu.VMEM((total, width), jnp.bfloat16),
            pltpu.SemaphoreType.DMA,
        ],
        compiler_params=PARAMS,
        name="first_qkv",
    )(unit, *mods, weight_qk, pltpu.with_memory_space_constraint(weight, pltpu.HBM), stale)


def second_kernel(
    mod_ref, wqk_ref, wv_ref, kv_0_ref, *refs, rows
):
    mine_refs, other_refs, before_refs = (refs[i * CHUNKS : (i + 1) * CHUNKS] for i in range(3))
    o_ref, kv_ref, *base_refs, normed_ref = refs[3 * CHUNKS :]
    total, span = mine_refs[0].shape
    half = span * CHUNKS
    core = lax.axis_index("mp") % 2
    pieces = [
        (ref, pl.ds(pl.multiple_of(index * half + chunk * span, LANES), span))
        for refs, index in ((mine_refs, core), (other_refs, 1 - core))
        for chunk, ref in enumerate(refs)
    ]
    step = 16
    for start in range(0, total, step):
        line = slice(start, start + step)
        values = [ref[line, :].astype(jnp.float32) for ref, _ in pieces]
        mean = sum(jnp.sum(value, axis=-1, keepdims=True) for value in values) / (2 * half)
        values = [value - mean for value in values]
        spread = sum(jnp.sum(value * value, axis=-1, keepdims=True) for value in values) / (2 * half)
        inverse = lax.rsqrt(spread + EPS)
        for value, (_, at) in zip(values, pieces):
            normed = value * inverse * (1.0 + mod_ref[1:2, at]) + mod_ref[0:1, at]
            normed_ref[line, at] = normed.astype(jnp.bfloat16)
    project(normed_ref, wqk_ref, wv_ref, o_ref, kv_ref, rows)
    is_first = lax.axis_index("section") == 0

    @pl.when(is_first)
    def _():
        kv_ref[...] = kv_0_ref[...]
        for base_ref, before_ref in zip(base_refs, before_refs):
            base_ref[...] = before_ref[...]

    @pl.when(jnp.logical_not(is_first))
    def _():
        for base_ref, mine_ref in zip(base_refs, mine_refs):
            base_ref[...] = mine_ref[...]


def second_call(mine, other, before, kv_0, mod, weight_qk, weight_v, rows, devices):
    total, span = mine[0].shape
    return pl.pallas_call(
        lambda *refs: second_kernel(*refs, rows=rows),
        out_shape=(
            jax.ShapeDtypeStruct((devices, 3 * rows, LANES), jnp.bfloat16),
            jax.ShapeDtypeStruct(kv_0.shape, jnp.bfloat16),
        )
        + (pltpu.VMEM((total, span), jnp.bfloat16),) * CHUNKS,
        in_specs=[VMEM] * (4 + 3 * CHUNKS),
        out_specs=(VMEM,) * (2 + CHUNKS),
        scratch_shapes=[pltpu.VMEM((total, 2 * CHUNKS * span), jnp.bfloat16)],
        compiler_params=PARAMS,
        name="second_qkv",
    )(mod, weight_qk, weight_v, kv_0, *mine, *other, *before)


def attention_kernel(*refs, rows, per_dev, patches, blocks):
    if len(refs) == 8:
        lens_ref, text_ref, recv_ref, stale_ref, w_ref, o_ref, w_vmem, sem = refs
        copy = pltpu.make_async_copy(w_ref, w_vmem, sem)
        copy.start()
    else:
        lens_ref, text_ref, recv_ref, stale_ref, o_ref = refs
        copy = None
    devices = recv_ref.shape[0]
    capacity = devices * per_dev

    def block(ref, base, index):
        start = base + index * per_dev
        return ref[:, start : start + per_dev, :].reshape(capacity, LANES)

    groups = patches + 1
    fresh_k = [block(recv_ref, rows, index) for index in range(groups)]
    fresh_v = [block(recv_ref, 2 * rows, index) for index in range(groups)]
    stale_base = 3 * rows
    stale_k = [None] + [block(stale_ref, stale_base, index) for index in range(patches - 1)]
    stale_base += (patches - 1) * per_dev
    stale_v = [None] + [block(stale_ref, stale_base, index) for index in range(patches - 1)]
    slot = lax.broadcasted_iota(jnp.int32, (1, groups * capacity), 1)
    limit = jnp.zeros((1, groups * capacity), jnp.int32)
    request = jnp.minimum(lax.axis_index("seq") // blocks, lens_ref.shape[0] - 1)
    for index in range(groups):
        length = lens_ref[request, index] if index < patches else text_ref[request]
        limit = jnp.where(slot >= index * capacity, length + index * capacity, limit)
    bias = jnp.where(slot < limit, 0.0, NEG)
    lane = lax.broadcasted_iota(jnp.int32, (1, LANES), 1)
    ones = jnp.ones((groups * capacity, LANES), jnp.bfloat16)
    factor = HEAD ** (-0.5) * math.log2(math.e)
    for patch in range(patches):
        keys = jnp.concatenate(
            [fresh_k[i] if i <= patch else stale_k[i] for i in range(patches)] + [fresh_k[patches]], axis=0
        )
        values = jnp.concatenate(
            [fresh_v[i] if i <= patch else stale_v[i] for i in range(patches)] + [fresh_v[patches]], axis=0
        )
        members = [patch, patches] if patch == 0 else [patch]
        queries = [block(recv_ref, 0, group) for group in members]
        queries = [jnp.where(lane < HEAD, q, jnp.zeros_like(q)) for q in queries] + [
            jnp.where(lane < HEAD, jnp.zeros_like(q), q) for q in queries
        ]
        scores = lax.dot_general(
            jnp.concatenate(queries, axis=0),
            keys,
            (((1,), (1,)), ((), ())),
            preferred_element_type=jnp.float32,
        )
        scores = scores * factor + bias
        top = jnp.max(scores, axis=-1, keepdims=True)
        weights = jnp.exp2(scores - top).astype(jnp.bfloat16)
        acc = jnp.dot(weights, jnp.concatenate([values, ones], axis=1), preferred_element_type=jnp.float32)
        acc = acc[:, :LANES] / acc[:, LANES:]
        for index, group in enumerate(members):
            lower = acc[index * capacity : (index + 1) * capacity]
            upper = acc[(len(members) + index) * capacity : (len(members) + index + 1) * capacity]
            out = jnp.where(lane < HEAD, lower, upper).astype(jnp.bfloat16)
            start = group * per_dev
            o_ref[:, start : start + per_dev, :] = out.reshape(devices, per_dev, LANES)
    if copy is not None:
        copy.wait()


def attention_call(lens, text_len, recv, stale, weight, rows, per_dev, blocks):
    devices = recv.shape[0]
    outs = jax.ShapeDtypeStruct((devices, rows, LANES), jnp.bfloat16)
    loads = weight is not None
    return pl.pallas_call(
        lambda *refs: attention_kernel(*refs, rows=rows, per_dev=per_dev, patches=lens.shape[1], blocks=blocks),
        out_shape=(outs, pltpu.VMEM(weight.shape, weight.dtype)) if loads else outs,
        in_specs=[SMEM, SMEM, VMEM, VMEM] + ([ANY] if loads else []),
        out_specs=(VMEM, VMEM) if loads else VMEM,
        scratch_shapes=[pltpu.SemaphoreType.DMA] if loads else [],
        compiler_params=PARAMS,
        name="attention",
    )(lens, text_len, recv, stale, *([pltpu.with_memory_space_constraint(weight, pltpu.HBM)] if loads else []))


def out_kernel(recv_ref, mod_ref, w_ref, *refs, mine, last):
    *refs, mixed_ref = refs
    depth, width = w_ref.shape
    rows = recv_ref.shape[1]
    blocks = depth // LANES
    for request in range(mixed_ref.shape[0] // rows):
        for block in range(blocks):
            mixed_ref[request * rows : (request + 1) * rows, block * LANES : (block + 1) * LANES] = recv_ref[
                request * blocks + block
            ]
    half = width // 2
    span = half // len(refs)
    core = lax.axis_index("mp") % 2
    index = core if mine else 1 - core
    for chunk, ref in enumerate(refs):
        at = pl.ds(pl.multiple_of(index * half + chunk * span, LANES), span)
        acc = jnp.dot(mixed_ref[...], w_ref[:, at], preferred_element_type=jnp.float32)
        acc = acc * mod_ref[2:3, at]
        if last:
            acc = jnp.where(lax.axis_index("section") == 0, jnp.zeros_like(acc), acc)
        ref[...] = acc.astype(ref.dtype)


def out_call(recv, mod, weight, requests, mine, last):
    depth, width = weight.shape
    total = requests * recv.shape[1]
    return pl.pallas_call(
        lambda *refs: out_kernel(*refs, mine=mine, last=last),
        out_shape=[
            pltpu.VMEM((total, width // 2 // CHUNKS), jnp.float32 if mine else jnp.bfloat16)
            for _ in range(CHUNKS)
        ],
        in_specs=[VMEM, VMEM, VMEM],
        out_specs=[VMEM] * CHUNKS,
        scratch_shapes=[pltpu.VMEM((total, depth), jnp.bfloat16)],
        compiler_params=PARAMS,
        name="out_projection",
    )(recv, mod, weight)


def pick_kernel(arrived_ref, own_ref, o_ref):
    @pl.when(lax.axis_index("section") == 0)
    def _():
        o_ref[...] = own_ref[...]

    @pl.when(lax.axis_index("section") != 0)
    def _():
        o_ref[...] = arrived_ref[...]


def pick_call(arrived, own):
    return pl.pallas_call(
        pick_kernel,
        out_shape=pltpu.VMEM(own.shape, own.dtype),
        in_specs=[VMEM, VMEM],
        out_specs=VMEM,
        compiler_params=PARAMS,
        name="pick",
    )(arrived, own)


def cache_kernel(kv_ref, video_ref, text_ref):
    _, requests, patches, per_dev, _, _ = video_ref.shape
    row = 0
    for request in range(requests):
        for patch in range(patches + 1):
            for kind in range(2):
                values = kv_ref[kind, row : row + per_dev, :]
                if patch < patches:
                    video_ref[0, request, patch, :, kind, :] = values
                else:
                    text_ref[0, request, :, kind, :] = values
            row += per_dev


def cache_call(kv, video_shape, requests):
    per_dev, columns = video_shape[3], video_shape[5]
    return pl.pallas_call(
        cache_kernel,
        out_shape=(
            jax.ShapeDtypeStruct(video_shape, jnp.bfloat16),
            jax.ShapeDtypeStruct((1, requests, per_dev, 2, columns), jnp.bfloat16),
        ),
        in_specs=[VMEM],
        out_specs=(VMEM, VMEM),
        compiler_params=PARAMS,
        name="cache",
    )(kv)


def store_kernel(*refs):
    *pieces, video_ref, text_ref, sems = refs
    patches = video_ref.shape[2]
    span = pieces[0].shape[-1]
    half = span * CHUNKS
    core = lax.axis_index("mp") % 2
    copies = []
    for side, source in enumerate(pieces):
        index = core if side < CHUNKS else 1 - core
        at = pl.ds(pl.multiple_of(index * half + side % CHUNKS * span, LANES), span)
        copies.append(
            pltpu.make_async_copy(
                source.at[:, pl.ds(0, patches)], video_ref.at[0, :, :, :, at], sems.at[side, 0]
            )
        )
        copies.append(pltpu.make_async_copy(source.at[:, patches], text_ref.at[0, :, :, at], sems.at[side, 1]))
    for copy in copies:
        copy.start()
    for copy in copies:
        copy.wait()


def store_call(mine, other, video_shape, text_shape):
    _, requests, patches, per_dev, _ = video_shape
    pieces = [piece.reshape(requests, patches + 1, per_dev, -1) for piece in mine + other]
    return pl.pallas_call(
        store_kernel,
        out_shape=(
            jax.ShapeDtypeStruct(video_shape, jnp.bfloat16),
            jax.ShapeDtypeStruct(text_shape, jnp.bfloat16),
        ),
        in_specs=[VMEM] * (2 * CHUNKS),
        out_specs=(ANY, ANY),
        scratch_shapes=[pltpu.SemaphoreType.DMA((2 * CHUNKS, 2))],
        compiler_params=PARAMS,
        name="store",
    )(*pieces)


def body(video, text, patch_lengths, text_len, timestep, w_mod, w_qkv, w_out, stale_cache):
    devices = lax.axis_size("seq")
    requests, patches, per_dev, _ = video.shape
    blocks = w_out.shape[1] // LANES
    rows = patches * per_dev + text.shape[1]

    own_mod = modulation(timestep, w_mod[0])
    mods = [own_mod] + [
        swap(own_mod, lambda section, part, flip=flip: (section, part ^ flip)) for flip in (1, 2, 3)
    ]
    weight = w_qkv[0].transpose(1, 0, 2)
    unit, stale, weight_qk, *x_half = prepare_call(video, text, weight, stale_cache[0])

    def reduced(mixed, weight_out, mod, last):
        others = each(swap_core, out_call(mixed, mod, weight_out, requests, False, last))
        mines = out_call(mixed, mod, weight_out, requests, True, last)
        return [(a + b.astype(jnp.float32)).astype(jnp.bfloat16) for a, b in zip(mines, others)]

    def added(x_half, on_chip, arrived):
        return [
            (a.astype(jnp.float32) + (b.astype(jnp.float32) + c.astype(jnp.float32))).astype(jnp.bfloat16)
            for a, b, c in zip(x_half, on_chip, arrived)
        ]

    def each(function, values):
        return [function(value) for value in values]

    sent_0, kv_0, mod, weight_v = first_call(unit, mods, weight_qk, weight, stale, rows, devices)
    recv_0 = lax.all_to_all(sent_0, "seq", 0, 0, tiled=True)
    weight_out = w_out[0]
    attended = attention_call(patch_lengths, text_len, recv_0, recv_0, None, rows, per_dev, blocks)
    on_chip = reduced(lax.all_to_all(attended, "seq", 0, 0, tiled=True), weight_out, mod, False)
    crossed = pick_call(next_section(on_chip[0]), on_chip[0])
    result_0 = added(x_half, [crossed, on_chip[1]], [swap_chip(crossed), swap_chip(on_chip[1])])

    x_half = [result_0[0], next_section(result_0[1])]
    sent_1, key_value, *base = second_call(
        x_half, each(swap_core, x_half), result_0, kv_0, mod, weight_qk, weight_v, rows, devices
    )
    recv_1 = lax.all_to_all(sent_1, "seq", 0, 0, tiled=True)
    attended = attention_call(patch_lengths, text_len, recv_1, recv_0, None, rows, per_dev, blocks)
    on_chip = reduced(lax.all_to_all(attended, "seq", 0, 0, tiled=True), weight_out, mod, True)
    arrived = each(swap_chip, on_chip)
    arrived[0], key_value = lax.optimization_barrier((arrived[0], key_value))

    cache_video, cache_text = cache_call(key_value, (1,) + stale_cache.shape[1:], requests)
    result = added(base, on_chip, arrived)
    hidden_video, hidden_text = store_call(result, each(swap_core, result), (1,) + video.shape, (1,) + text.shape)
    return (hidden_video, hidden_text, cache_video, cache_text)


def solution(mesh):
    placed = (
        P(None, None, "seq", None),
        P(None, "seq", None),
        P(),
        P(),
        P(),
        P("section", None, "mp"),
        P("section", None, None, "mp"),
        P("section", "mp", None),
        P("section", None, None, "seq", None, "mp"),
    )
    return jax.shard_map(
        body,
        mesh=mesh,
        in_specs=placed,
        out_specs=(
            P("section", None, None, "seq", None),
            P("section", None, "seq", None),
            P("section", None, None, "seq", None, "mp"),
            P("section", None, "seq", None, "mp"),
        ),
        check_vma=False,
    )
```

```python
import math

import jax
import jax.numpy as jnp
from jax import lax
from jax.experimental import pallas as pl
from jax.experimental.pallas import tpu as pltpu
from jax.sharding import PartitionSpec as P

HEAD = 64
LANES = 128
EPS = 1e-05
NEG = -1e30
CHUNKS = 2
WIDE = 256
VMEM_LIMIT = 12 * 1024 * 1024


def modulation(timestep, weight):
    half_width = weight.shape[0] // 2
    frequency = jnp.exp(-math.log(10000.0) * jnp.arange(half_width, dtype=jnp.float32) / half_width)
    phases = timestep.astype(jnp.float32)[0] * frequency
    embedding = jnp.concatenate([jnp.cos(phases), jnp.sin(phases)])
    active = jax.nn.silu(embedding).astype(jnp.bfloat16)
    return jnp.dot(active[None, :], weight, preferred_element_type=jnp.float32)


def swap(value, mapping):
    pairs = []
    for section in range(2):
        for part in range(4):
            target = mapping(section, part)
            pairs.append((section * 4 + part, target[0] * 4 + target[1]))
    return lax.ppermute(value, ("section", "mp"), pairs)


def swap_core(value):
    return swap(value, lambda section, part: (section, part ^ 1))


def swap_chip(value):
    return swap(value, lambda section, part: (section, part ^ 2))


def next_section(value):
    return swap(value, lambda section, part: (1 - section, part ^ 2))

VMEM = pl.BlockSpec(memory_space=pltpu.VMEM)
SMEM = pl.BlockSpec(memory_space=pltpu.SMEM)
ANY = pl.BlockSpec(memory_space=pl.ANY)
PARAMS = pltpu.CompilerParams(vmem_limit_bytes=VMEM_LIMIT)


def centered(values):
    values = values.astype(jnp.float32)
    center = values - jnp.mean(values, axis=-1, keepdims=True)
    spread = jnp.mean(center * center, axis=-1, keepdims=True)
    return center * lax.rsqrt(spread + EPS)


def prepare_kernel(
    video_ref, text_ref, w_ref, stale_ref, unit_ref, packed_ref, w_vmem, *refs
):
    *half_refs, video_buf, text_buf, stale_buf, x_ref, sems = refs
    requests, patches, per_dev, width = video_ref.shape
    first = [
        pltpu.make_async_copy(stale_ref, stale_buf, sems.at[0]),
        pltpu.make_async_copy(video_ref, video_buf, sems.at[1]),
        pltpu.make_async_copy(text_ref, text_buf, sems.at[2]),
    ]
    load = pltpu.make_async_copy(w_ref.at[pl.ds(0, 2)], w_vmem, sems.at[3])
    for copy in first + [load]:
        copy.start()
    first[0].wait()
    blocks = w_ref.shape[2] // LANES
    for request in range(requests):
        for patch in range(1, patches):
            both = stale_buf[request, patch]
            for kind in range(2):
                values = both[:, kind, :]
                row = (kind * (patches - 1) + patch - 1) * per_dev
                for block in range(blocks):
                    packed_ref[request * blocks + block, row : row + per_dev, :] = values[
                        :, block * LANES : (block + 1) * LANES
                    ]
    for copy in first[1:]:
        copy.wait()
    row = 0
    for request in range(requests):
        for patch in range(patches + 1):
            values = video_buf[request, patch] if patch < patches else text_buf[request]
            x_ref[row : row + per_dev, :] = values
            unit_ref[row : row + per_dev, :] = centered(values)
            row += per_dev
    half = width // 2
    core = lax.axis_index("mp") % 2
    span = half // len(half_refs)
    for chunk, ref in enumerate(half_refs):
        ref[...] = x_ref[:, pl.ds(pl.multiple_of(core * half + chunk * span, LANES), span)]
    load.wait()


def prepare_call(video, text, weight, stale):
    requests, patches, per_dev, width = video.shape
    total = requests * (patches + 1) * per_dev
    units = requests * (weight.shape[2] // LANES)
    operands = [pltpu.with_memory_space_constraint(value, pltpu.HBM) for value in (video, text, weight, stale)]
    return pl.pallas_call(
        prepare_kernel,
        out_shape=(
            pltpu.VMEM((total, width), jnp.float32),
            pltpu.VMEM((units, 2 * (patches - 1) * per_dev, LANES), jnp.bfloat16),
            pltpu.VMEM((2,) + weight.shape[1:], jnp.bfloat16),
        )
        + (pltpu.VMEM((total, width // 2 // CHUNKS), jnp.bfloat16),) * CHUNKS,
        in_specs=[ANY] * 4,
        out_specs=(VMEM,) * (3 + CHUNKS),
        scratch_shapes=[
            pltpu.VMEM(video.shape, jnp.bfloat16),
            pltpu.VMEM(text.shape, jnp.bfloat16),
            pltpu.VMEM(stale.shape, jnp.bfloat16),
            pltpu.VMEM((total, width), jnp.bfloat16),
            pltpu.SemaphoreType.DMA((4,)),
        ],
        compiler_params=PARAMS,
        name="prepare",
    )(*operands)


def project(normed_ref, wqk_ref, wv_ref, o_ref, kv_ref, rows, loads=()):
    columns = wv_ref.shape[1]
    blocks = columns // LANES
    requests = normed_ref.shape[0] // rows
    for unit in range(requests * blocks, o_ref.shape[0]):
        o_ref[unit] = jnp.zeros(o_ref.shape[1:], o_ref.dtype)
    for part in range(3):
        for wide in range(0, columns, WIDE):
            at = slice(wide, wide + WIDE)
            if part == 2 and loads:
                loads[wide // WIDE].wait()
            weight = wqk_ref[part, :, at] if part < 2 else wv_ref[:, at]
            acc = jnp.dot(normed_ref[...], weight, preferred_element_type=jnp.float32).astype(jnp.bfloat16)
            if part:
                kv_ref[part - 1, :, at] = acc
            for request in range(requests):
                for block in range(WIDE // LANES):
                    unit = request * blocks + wide // LANES + block
                    o_ref[unit, part * rows : (part + 1) * rows, :] = acc[
                        request * rows : (request + 1) * rows, block * LANES : (block + 1) * LANES
                    ]


def first_kernel(
    unit_ref,
    mod_0,
    mod_1,
    mod_2,
    mod_3,
    wqk_ref,
    w_ref,
    stale_ref,
    o_ref,
    kv_ref,
    mod_ref,
    wv_ref,
    pieces_ref,
    normed_ref,
    sems,
    *,
    rows,
):
    loads = []
    for index in range(wv_ref.shape[1] // WIDE):
        at = pl.ds(index * WIDE, WIDE)
        copy = pltpu.make_async_copy(w_ref.at[2, :, at], wv_ref.at[:, at], sems.at[index])
        copy.start()
        loads.append(copy)
    for index, piece in enumerate((mod_0, mod_1, mod_2, mod_3)):
        pieces_ref[lax.axis_index("mp") ^ index, 0:1, :] = piece[...]
    total, width = unit_ref.shape
    piece_width = mod_0.shape[1]
    for line in range(3):
        start = line * width
        while start < (line + 1) * width:
            slot, at = divmod(start, piece_width)
            count = min(piece_width - at, (line + 1) * width - start)
            to = start - line * width
            mod_ref[line : line + 1, to : to + count] = pieces_ref[slot, 0:1, at : at + count]
            start += count
    step = 16
    for start in range(0, total, step):
        normed = unit_ref[start : start + step, :] * (1.0 + mod_ref[1:2, :]) + mod_ref[0:1, :]
        normed_ref[start : start + step, :] = normed.astype(jnp.bfloat16)
    for unit in range(stale_ref.shape[0]):
        o_ref[unit, 3 * rows :, :] = stale_ref[unit]
    project(normed_ref, wqk_ref, wv_ref, o_ref, kv_ref, rows, loads)


def first_call(unit, mods, weight_qk, weight, stale, rows, devices):
    total, width = unit.shape
    return pl.pallas_call(
        lambda *refs: first_kernel(*refs, rows=rows),
        out_shape=(
            jax.ShapeDtypeStruct((devices, 3 * rows + stale.shape[1], LANES), jnp.bfloat16),
            jax.ShapeDtypeStruct((2, total, weight.shape[2]), jnp.bfloat16),
            pltpu.VMEM((3, width), jnp.float32),
            pltpu.VMEM(weight.shape[1:], jnp.bfloat16),
        ),
        in_specs=[VMEM] * 6 + [ANY, VMEM],
        out_specs=(VMEM,) * 4,
        scratch_shapes=[
            pltpu.VMEM((4, 8, mods[0].shape[1]), jnp.float32),
            pltpu.VMEM((total, width), jnp.bfloat16),
            pltpu.SemaphoreType.DMA((weight.shape[2] // WIDE,)),
        ],
        compiler_params=PARAMS,
        name="first_qkv",
    )(unit, *mods, weight_qk, pltpu.with_memory_space_constraint(weight, pltpu.HBM), stale)


def second_kernel(
    mod_ref, wqk_ref, wv_ref, kv_0_ref, *refs, rows
):
    mine_refs, other_refs, before_refs = (refs[i * CHUNKS : (i + 1) * CHUNKS] for i in range(3))
    o_ref, kv_ref, *base_refs, normed_ref = refs[3 * CHUNKS :]
    total, span = mine_refs[0].shape
    half = span * CHUNKS
    core = lax.axis_index("mp") % 2
    pieces = [
        (ref, pl.ds(pl.multiple_of(index * half + chunk * span, LANES), span))
        for refs, index in ((mine_refs, core), (other_refs, 1 - core))
        for chunk, ref in enumerate(refs)
    ]
    step = 16
    for start in range(0, total, step):
        line = slice(start, start + step)
        values = [ref[line, :].astype(jnp.float32) for ref, _ in pieces]
        mean = sum(jnp.sum(value, axis=-1, keepdims=True) for value in values) / (2 * half)
        values = [value - mean for value in values]
        spread = sum(jnp.sum(value * value, axis=-1, keepdims=True) for value in values) / (2 * half)
        inverse = lax.rsqrt(spread + EPS)
        for value, (_, at) in zip(values, pieces):
            normed = value * inverse * (1.0 + mod_ref[1:2, at]) + mod_ref[0:1, at]
            normed_ref[line, at] = normed.astype(jnp.bfloat16)
    project(normed_ref, wqk_ref, wv_ref, o_ref, kv_ref, rows)
    is_first = lax.axis_index("section") == 0

    @pl.when(is_first)
    def _():
        kv_ref[...] = kv_0_ref[...]
        for base_ref, before_ref in zip(base_refs, before_refs):
            base_ref[...] = before_ref[...]

    @pl.when(jnp.logical_not(is_first))
    def _():
        for base_ref, mine_ref in zip(base_refs, mine_refs):
            base_ref[...] = mine_ref[...]


def second_call(mine, other, before, kv_0, mod, weight_qk, weight_v, rows, devices):
    total, span = mine[0].shape
    return pl.pallas_call(
        lambda *refs: second_kernel(*refs, rows=rows),
        out_shape=(
            jax.ShapeDtypeStruct((devices, 3 * rows, LANES), jnp.bfloat16),
            jax.ShapeDtypeStruct(kv_0.shape, jnp.bfloat16),
        )
        + (pltpu.VMEM((total, span), jnp.bfloat16),) * CHUNKS,
        in_specs=[VMEM] * (4 + 3 * CHUNKS),
        out_specs=(VMEM,) * (2 + CHUNKS),
        scratch_shapes=[pltpu.VMEM((total, 2 * CHUNKS * span), jnp.bfloat16)],
        compiler_params=PARAMS,
        name="second_qkv",
    )(mod, weight_qk, weight_v, kv_0, *mine, *other, *before)


def attention_kernel(*refs, rows, per_dev, patches, blocks):
    if len(refs) == 8:
        lens_ref, text_ref, recv_ref, stale_ref, w_ref, o_ref, w_vmem, sem = refs
        copy = pltpu.make_async_copy(w_ref, w_vmem, sem)
        copy.start()
    else:
        lens_ref, text_ref, recv_ref, stale_ref, o_ref = refs
        copy = None
    devices = recv_ref.shape[0]
    capacity = devices * per_dev

    def block(ref, base, index):
        start = base + index * per_dev
        return ref[:, start : start + per_dev, :].reshape(capacity, LANES)

    groups = patches + 1
    fresh_k = [block(recv_ref, rows, index) for index in range(groups)]
    fresh_v = [block(recv_ref, 2 * rows, index) for index in range(groups)]
    stale_base = 3 * rows
    stale_k = [None] + [block(stale_ref, stale_base, index) for index in range(patches - 1)]
    stale_base += (patches - 1) * per_dev
    stale_v = [None] + [block(stale_ref, stale_base, index) for index in range(patches - 1)]
    slot = lax.broadcasted_iota(jnp.int32, (1, groups * capacity), 1)
    limit = jnp.zeros((1, groups * capacity), jnp.int32)
    request = jnp.minimum(lax.axis_index("seq") // blocks, lens_ref.shape[0] - 1)
    for index in range(groups):
        length = lens_ref[request, index] if index < patches else text_ref[request]
        limit = jnp.where(slot >= index * capacity, length + index * capacity, limit)
    bias = jnp.where(slot < limit, 0.0, NEG)
    lane = lax.broadcasted_iota(jnp.int32, (1, LANES), 1)
    ones = jnp.ones((groups * capacity, LANES), jnp.bfloat16)
    factor = HEAD ** (-0.5) * math.log2(math.e)
    for patch in range(patches):
        keys = jnp.concatenate(
            [fresh_k[i] if i <= patch else stale_k[i] for i in range(patches)] + [fresh_k[patches]], axis=0
        )
        values = jnp.concatenate(
            [fresh_v[i] if i <= patch else stale_v[i] for i in range(patches)] + [fresh_v[patches]], axis=0
        )
        members = [patch, patches] if patch == 0 else [patch]
        queries = [block(recv_ref, 0, group) for group in members]
        queries = [jnp.where(lane < HEAD, q, jnp.zeros_like(q)) for q in queries] + [
            jnp.where(lane < HEAD, jnp.zeros_like(q), q) for q in queries
        ]
        scores = lax.dot_general(
            jnp.concatenate(queries, axis=0),
            keys,
            (((1,), (1,)), ((), ())),
            preferred_element_type=jnp.float32,
        )
        scores = scores * factor + bias
        top = jnp.max(scores, axis=-1, keepdims=True)
        weights = jnp.exp2(scores - top).astype(jnp.bfloat16)
        acc = jnp.dot(weights, jnp.concatenate([values, ones], axis=1), preferred_element_type=jnp.float32)
        acc = acc[:, :LANES] / acc[:, LANES:]
        for index, group in enumerate(members):
            lower = acc[index * capacity : (index + 1) * capacity]
            upper = acc[(len(members) + index) * capacity : (len(members) + index + 1) * capacity]
            out = jnp.where(lane < HEAD, lower, upper).astype(jnp.bfloat16)
            start = group * per_dev
            o_ref[:, start : start + per_dev, :] = out.reshape(devices, per_dev, LANES)
    if copy is not None:
        copy.wait()


def attention_call(lens, text_len, recv, stale, weight, rows, per_dev, blocks):
    devices = recv.shape[0]
    outs = jax.ShapeDtypeStruct((devices, rows, LANES), jnp.bfloat16)
    loads = weight is not None
    return pl.pallas_call(
        lambda *refs: attention_kernel(*refs, rows=rows, per_dev=per_dev, patches=lens.shape[1], blocks=blocks),
        out_shape=(outs, pltpu.VMEM(weight.shape, weight.dtype)) if loads else outs,
        in_specs=[SMEM, SMEM, VMEM, VMEM] + ([ANY] if loads else []),
        out_specs=(VMEM, VMEM) if loads else VMEM,
        scratch_shapes=[pltpu.SemaphoreType.DMA] if loads else [],
        compiler_params=PARAMS,
        name="attention",
    )(lens, text_len, recv, stale, *([pltpu.with_memory_space_constraint(weight, pltpu.HBM)] if loads else []))


def out_kernel(recv_ref, mod_ref, w_ref, *refs, mine, last):
    *refs, mixed_ref = refs
    depth, width = w_ref.shape
    rows = recv_ref.shape[1]
    blocks = depth // LANES
    for request in range(mixed_ref.shape[0] // rows):
        for block in range(blocks):
            mixed_ref[request * rows : (request + 1) * rows, block * LANES : (block + 1) * LANES] = recv_ref[
                request * blocks + block
            ]
    half = width // 2
    span = half // len(refs)
    core = lax.axis_index("mp") % 2
    index = core if mine else 1 - core
    for chunk, ref in enumerate(refs):
        at = pl.ds(pl.multiple_of(index * half + chunk * span, LANES), span)
        acc = jnp.dot(mixed_ref[...], w_ref[:, at], preferred_element_type=jnp.float32)
        acc = acc * mod_ref[2:3, at]
        if last:
            acc = jnp.where(lax.axis_index("section") == 0, jnp.zeros_like(acc), acc)
        ref[...] = acc.astype(ref.dtype)


def out_call(recv, mod, weight, requests, mine, last):
    depth, width = weight.shape
    total = requests * recv.shape[1]
    return pl.pallas_call(
        lambda *refs: out_kernel(*refs, mine=mine, last=last),
        out_shape=[
            pltpu.VMEM((total, width // 2 // CHUNKS), jnp.float32 if mine else jnp.bfloat16)
            for _ in range(CHUNKS)
        ],
        in_specs=[VMEM, VMEM, VMEM],
        out_specs=[VMEM] * CHUNKS,
        scratch_shapes=[pltpu.VMEM((total, depth), jnp.bfloat16)],
        compiler_params=PARAMS,
        name="out_projection",
    )(recv, mod, weight)


def pick_kernel(arrived_ref, own_ref, o_ref):
    @pl.when(lax.axis_index("section") == 0)
    def _():
        o_ref[...] = own_ref[...]

    @pl.when(lax.axis_index("section") != 0)
    def _():
        o_ref[...] = arrived_ref[...]


def pick_call(arrived, own):
    return pl.pallas_call(
        pick_kernel,
        out_shape=pltpu.VMEM(own.shape, own.dtype),
        in_specs=[VMEM, VMEM],
        out_specs=VMEM,
        compiler_params=PARAMS,
        name="pick",
    )(arrived, own)


def cache_kernel(kv_ref, video_ref, text_ref):
    _, requests, patches, per_dev, _, _ = video_ref.shape
    row = 0
    for request in range(requests):
        for patch in range(patches + 1):
            for kind in range(2):
                values = kv_ref[kind, row : row + per_dev, :]
                if patch < patches:
                    video_ref[0, request, patch, :, kind, :] = values
                else:
                    text_ref[0, request, :, kind, :] = values
            row += per_dev


def cache_call(kv, video_shape, requests):
    per_dev, columns = video_shape[3], video_shape[5]
    return pl.pallas_call(
        cache_kernel,
        out_shape=(
            jax.ShapeDtypeStruct(video_shape, jnp.bfloat16),
            jax.ShapeDtypeStruct((1, requests, per_dev, 2, columns), jnp.bfloat16),
        ),
        in_specs=[VMEM],
        out_specs=(VMEM, VMEM),
        compiler_params=PARAMS,
        name="cache",
    )(kv)


def store_kernel(*refs):
    *pieces, video_ref, text_ref, sems = refs
    patches = video_ref.shape[2]
    span = pieces[0].shape[-1]
    half = span * CHUNKS
    core = lax.axis_index("mp") % 2
    copies = []
    for side, source in enumerate(pieces):
        index = core if side < CHUNKS else 1 - core
        at = pl.ds(pl.multiple_of(index * half + side % CHUNKS * span, LANES), span)
        copies.append(
            pltpu.make_async_copy(
                source.at[:, pl.ds(0, patches)], video_ref.at[0, :, :, :, at], sems.at[side, 0]
            )
        )
        copies.append(pltpu.make_async_copy(source.at[:, patches], text_ref.at[0, :, :, at], sems.at[side, 1]))
    for copy in copies:
        copy.start()
    for copy in copies:
        copy.wait()


def store_call(mine, other, video_shape, text_shape):
    _, requests, patches, per_dev, _ = video_shape
    pieces = [piece.reshape(requests, patches + 1, per_dev, -1) for piece in mine + other]
    return pl.pallas_call(
        store_kernel,
        out_shape=(
            jax.ShapeDtypeStruct(video_shape, jnp.bfloat16),
            jax.ShapeDtypeStruct(text_shape, jnp.bfloat16),
        ),
        in_specs=[VMEM] * (2 * CHUNKS),
        out_specs=(ANY, ANY),
        scratch_shapes=[pltpu.SemaphoreType.DMA((2 * CHUNKS, 2))],
        compiler_params=PARAMS,
        name="store",
    )(*pieces)


def body(video, text, patch_lengths, text_len, timestep, w_mod, w_qkv, w_out, stale_cache):
    devices = lax.axis_size("seq")
    requests, patches, per_dev, _ = video.shape
    blocks = w_out.shape[1] // LANES
    rows = patches * per_dev + text.shape[1]

    own_mod = modulation(timestep, w_mod[0])
    mods = [own_mod] + [
        swap(own_mod, lambda section, part, flip=flip: (section, part ^ flip)) for flip in (1, 2, 3)
    ]
    weight = w_qkv[0].transpose(1, 0, 2)
    unit, stale, weight_qk, *x_half = prepare_call(video, text, weight, stale_cache[0])

    def reduced(mixed, weight_out, mod, last):
        others = each(swap_core, out_call(mixed, mod, weight_out, requests, False, last))
        mines = out_call(mixed, mod, weight_out, requests, True, last)
        return [(a + b.astype(jnp.float32)).astype(jnp.bfloat16) for a, b in zip(mines, others)]

    def added(x_half, on_chip, arrived):
        return [
            (a.astype(jnp.float32) + (b.astype(jnp.float32) + c.astype(jnp.float32))).astype(jnp.bfloat16)
            for a, b, c in zip(x_half, on_chip, arrived)
        ]

    def each(function, values):
        return [function(value) for value in values]

    sent_0, kv_0, mod, weight_v = first_call(unit, mods, weight_qk, weight, stale, rows, devices)
    recv_0 = lax.all_to_all(sent_0, "seq", 0, 0, tiled=True)
    weight_out = w_out[0]
    attended = attention_call(patch_lengths, text_len, recv_0, recv_0, None, rows, per_dev, blocks)
    on_chip = reduced(lax.all_to_all(attended, "seq", 0, 0, tiled=True), weight_out, mod, False)
    crossed = pick_call(next_section(on_chip[0]), on_chip[0])
    result_0 = added(x_half, [crossed, on_chip[1]], [swap_chip(crossed), swap_chip(on_chip[1])])

    x_half = [result_0[0], next_section(result_0[1])]
    sent_1, key_value, *base = second_call(
        x_half, each(swap_core, x_half), result_0, kv_0, mod, weight_qk, weight_v, rows, devices
    )
    recv_1 = lax.all_to_all(sent_1, "seq", 0, 0, tiled=True)
    attended = attention_call(patch_lengths, text_len, recv_1, recv_0, None, rows, per_dev, blocks)
    on_chip = reduced(lax.all_to_all(attended, "seq", 0, 0, tiled=True), weight_out, mod, True)
    arrived = each(swap_chip, on_chip)
    arrived[0], key_value = lax.optimization_barrier((arrived[0], key_value))

    cache_video, cache_text = cache_call(key_value, (1,) + stale_cache.shape[1:], requests)
    result = added(base, on_chip, arrived)
    hidden_video, hidden_text = store_call(result, each(swap_core, result), (1,) + video.shape, (1,) + text.shape)
    return (hidden_video, hidden_text, cache_video, cache_text)


def solution(mesh):
    placed = (
        P(None, None, "seq", None),
        P(None, "seq", None),
        P(),
        P(),
        P(),
        P("section", None, "mp"),
        P("section", None, None, "mp"),
        P("section", "mp", None),
        P("section", None, None, "seq", None, "mp"),
    )
    return jax.shard_map(
        body,
        mesh=mesh,
        in_specs=placed,
        out_specs=(
            P("section", None, None, "seq", None),
            P("section", None, "seq", None),
            P("section", None, None, "seq", None, "mp"),
            P("section", None, "seq", None, "mp"),
        ),
        check_vma=False,
    )
```
